32 devices in a mesh: ens: 2 (over y), node: 16 (over z, x, core).
Axes of the slice: x: 2, y: 2, z: 4, core: 2. Of those that a mesh axis runs over, the one named last changes fastest.
Arguments:
- hidden_embedding: bfloat16 [2, 16384, 1024], P('ens', 'node'), may hold values from -6 to 6
- random_perturbation: bfloat16 [2, 1024], P('ens'), may hold values from -3 to 3
- norm_gain: float32 [1024], replicated, may hold values from 0.5 to 1.5
- w_qkv: bfloat16 [1024, 3072], replicated, may hold values from -40 to 40
- w_proj: bfloat16 [1024, 1024], replicated, may hold values from -0.1875 to 0.1875
- w_fields: bfloat16 [1024, 100], replicated, may hold values from -0.1875 to 0.1875
- observed_reality: float32 [100, 16384], P(None, 'node'), may hold values from -6 to 6
- counts: int32 [16], replicated, may hold values from 512 to 1024, as said below
Outputs:
- predicted_outputs: bfloat16 [2, 100, 16384], P('ens', None, 'node')
- probabilistic_score: float32 [100, 16384], P(None, 'node')
- scaled_derivative: float32 [2, 100, 16384], P('ens', None, 'node')
The draws below stay inside these ranges and needn't reach their ends.
Inputs may be any that keep to these rules, and one draw needn't show every extreme that they name: `counts`: each shard has at least half of its 1024 slots live, its live nodes come first, one shard is full and one is exactly half full.
All inputs are finite; a program needn't handle non-finite values.
Results may differ from the reference program's by a relative error of at most 0.013.
The reference program's roundings to bfloat16 on the way count: a program that leaves them out, or rounds other values in their place, can miss the bound.
Values may be sent and summed in bfloat16 or wider, within the bound.
No kernel may reach another device: no remote copies, remote signals or barrier semaphores. Data moves between devices by JAX's collectives and lax.ppermute only.
A program may use at most 128 MiB of HBM per device.

```python
import jax
import jax.numpy as jnp
from jax import lax

C = 1024
HEADS = 16
HEAD_GROUP = 4
VARS = 100
NODE_SLOTS = 1024
HALF_WINDOW = 256
MEMBERS = 2
NODES = 16384
N_NODE = 16


def draw_counts(key, part):
    first, second, third = jax.random.split(jax.random.fold_in(key, 17), 3)
    values = jax.random.randint(first, (N_NODE,), NODE_SLOTS // 2, NODE_SLOTS + 1)
    full_at = jax.random.randint(second, (), 0, N_NODE)
    half_at = (full_at + 1 + jax.random.randint(third, (), 0, N_NODE - 1)) % N_NODE
    places = jnp.arange(N_NODE, dtype=jnp.int32)
    values = jnp.where(places == full_at, NODE_SLOTS, values)
    values = jnp.where(places == half_at, NODE_SLOTS // 2, values)
    return values.astype(jnp.int32)


def draw_hidden_embedding(key, part):
    first = jax.random.fold_in(jax.random.fold_in(key, 29), 0)
    base = jax.random.truncated_normal(first, -6.0, 6.0, (MEMBERS, NODES, C), jnp.float32)
    return base.astype(jnp.bfloat16)


def draw_w_qkv(key, part):
    first = jax.random.fold_in(jax.random.fold_in(key, 41), 0)
    scale = jnp.float32(C) ** (-0.5)
    whole = jax.random.truncated_normal(first, -6.0, 6.0, (C, 3 * C), jnp.float32) * scale
    return whole.astype(jnp.bfloat16)


def block_levels(key, shape, shards, low, largest):
    gain, own = 1.0, jax.random.fold_in(key, 6)
    for position, parts in shards:
        steps = jnp.exp(jax.random.uniform(jax.random.fold_in(own, position), (parts,), jnp.float32, low / len(shards), largest / len(shards)))
        gain = gain * jnp.repeat(steps, shape[position] // parts).reshape([-1 if axis == position else 1 for axis in range(len(shape))])
    return gain


def centred(key, dims, deviation, reach, cuts=(), held_as=jnp.bfloat16):
    values = deviation * jax.random.normal(key, dims, jnp.float32)
    if cuts:
        values = values * block_levels(key, dims, cuts, -0.22, 0.18)
    return jnp.clip(values, -reach, reach).astype(held_as)


def setup_inputs(seed: int = 0) -> dict:
    seeds = jax.random.split(jax.random.key(seed), 9)
    return {
        "hidden_embedding": draw_hidden_embedding(jax.random.fold_in(seeds[8], 71), 0),
        "random_perturbation": centred(seeds[1], (MEMBERS, C), 0.5, 3.0, ((0, 2),)),
        "norm_gain": jnp.clip(1.0 + 0.1 * jax.random.normal(seeds[2], (C,), jnp.float32), 0.5, 1.5),
        "w_qkv": draw_w_qkv(jax.random.fold_in(seeds[8], 71), 0),
        "w_proj": centred(seeds[4], (C, C), C ** -0.5, 0.1875),
        "w_fields": centred(seeds[5], (C, VARS), C ** -0.5, 0.1875),
        "observed_reality": centred(seeds[6], (VARS, NODES), 1.0, 6.0, ((1, 16),), jnp.float32),
        "counts": draw_counts(jax.random.fold_in(seeds[8], 71), 0),
    }


smooth_sq = 0.01
alpha_fair = 0.95

def attend(query, keys, values, allowed, heads, group):
    mem, rows, window_width = query.shape
    keyn = keys.shape[1]
    head_dim = window_width // heads
    groups = heads // group

    def split(arr, count):
        return jnp.moveaxis(arr.reshape(mem, count, groups, group, head_dim), 2, 1).reshape(mem * groups, count, group, head_dim)

    def one_group(item):
        q_part, k_part, v_part = item
        scores = jnp.einsum('qhd,khd->hqk', q_part.astype(jnp.float32), k_part.astype(jnp.float32)) / jnp.sqrt(jnp.float32(head_dim))
        scores = jnp.where(allowed[None], scores, jnp.float32(-1e+30))
        top = lax.optimization_barrier(jnp.max(scores, axis=-1, keepdims=True))
        expd = jnp.exp(scores - top)
        probs = (expd / lax.optimization_barrier(jnp.sum(expd, axis=-1, keepdims=True))).astype(jnp.bfloat16)
        return jnp.einsum('hqk,khd->qhd', probs.astype(jnp.float32), v_part.astype(jnp.float32)).astype(jnp.bfloat16)
    out = lax.map(one_group, (split(query, rows), split(keys, keyn), split(values, keyn)))
    out = jnp.moveaxis(out.reshape(mem, groups, rows, group, head_dim), 1, 2)
    return out.reshape(mem, rows, window_width)

def score_fragments(gridded_quantities, observed_reality, valid_flags):
    total = gridded_quantities.shape[0]

    def pair(row):
        diff = row[None] - gridded_quantities
        absd = jnp.sqrt(diff * diff + smooth_sq)
        return (lax.optimization_barrier(jnp.sum(absd, axis=0)), lax.optimization_barrier(jnp.sum(diff / absd, axis=0)))
    pair_sum, pair_grad = lax.map(pair, gridded_quantities)
    dtruth = gridded_quantities - observed_reality[None]
    atruth = jnp.sqrt(dtruth * dtruth + smooth_sq)
    eps_fair = (1.0 - alpha_fair) / total
    probabilistic_score = valid_flags[None] * (lax.optimization_barrier(jnp.mean(atruth, axis=0)) - (1.0 - eps_fair) / (2.0 * total * (total - 1)) * (lax.optimization_barrier(jnp.sum(pair_sum, axis=0)) - total * jnp.sqrt(jnp.float32(smooth_sq))))
    scaled_derivative = valid_flags[None, None] * (dtruth / atruth - (1.0 - eps_fair) / (total - 1) * pair_grad)
    return (probabilistic_score, scaled_derivative)

def reference(hidden_embedding, random_perturbation, norm_gain, w_qkv, w_proj, w_fields, observed_reality, counts):
    window_width = hidden_embedding.shape[2]
    slots = jnp.arange(NODES, dtype=jnp.int32)
    valid_flags = (slots % NODE_SLOTS < counts[slots // NODE_SLOTS]).astype(jnp.float32)
    live_pad = jnp.pad(valid_flags, (HALF_WINDOW, HALF_WINDOW))

    def lone_realisation(item):
        xrow, nrow = item
        x32 = xrow.astype(jnp.float32)
        mean = lax.optimization_barrier(jnp.mean(x32, axis=-1, keepdims=True))
        var = lax.optimization_barrier(jnp.mean((x32 - mean) ** 2, axis=-1, keepdims=True))
        normed = ((x32 - mean) * lax.rsqrt(var + 1e-05) * norm_gain[None] * (1.0 + nrow.astype(jnp.float32))[None]).astype(jnp.bfloat16)
        query_key_value = jnp.dot(normed, w_qkv, preferred_element_type=jnp.float32).astype(jnp.bfloat16)
        query = query_key_value[:, :window_width]
        kpad = jnp.pad(query_key_value[:, window_width:2 * window_width], ((HALF_WINDOW, HALF_WINDOW), (0, 0)))
        value_padded = jnp.pad(query_key_value[:, 2 * window_width:], ((HALF_WINDOW, HALF_WINDOW), (0, 0)))
        rel = jnp.arange(NODE_SLOTS + 2 * HALF_WINDOW, dtype=jnp.int32)[None, :] - HALF_WINDOW - jnp.arange(NODE_SLOTS, dtype=jnp.int32)[:, None]

        def shard(index):
            start_index = (index * NODE_SLOTS).astype(jnp.int32)
            q_rows = lax.dynamic_slice_in_dim(query, start_index, NODE_SLOTS, 0)
            k_rows = lax.dynamic_slice_in_dim(kpad, start_index, NODE_SLOTS + 2 * HALF_WINDOW, 0)
            value_rows = lax.dynamic_slice_in_dim(value_padded, start_index, NODE_SLOTS + 2 * HALF_WINDOW, 0)
            key_live = lax.dynamic_slice_in_dim(live_pad, start_index, NODE_SLOTS + 2 * HALF_WINDOW, 0)
            allowed = (rel >= -HALF_WINDOW) & (rel < HALF_WINDOW) & ((key_live[None, :] > 0.5) | (rel == 0))
            return attend(q_rows[None], k_rows[None], value_rows[None], allowed, HEADS, HEAD_GROUP)[0]
        attended = lax.map(shard, jnp.arange(N_NODE, dtype=jnp.int32)).reshape(NODES, window_width)
        updated = (x32 + jnp.dot(attended, w_proj, preferred_element_type=jnp.float32)).astype(jnp.bfloat16)
        gridded_quantities = jnp.dot(updated, w_fields, preferred_element_type=jnp.float32)
        return (gridded_quantities * valid_flags[:, None]).astype(jnp.bfloat16).T
    predicted_outputs = lax.map(lone_realisation, (hidden_embedding, random_perturbation))
    probabilistic_score, scaled_derivative = score_fragments(predicted_outputs.astype(jnp.float32), observed_reality, valid_flags)
    return (predicted_outputs, probabilistic_score, scaled_derivative)
```

```python
import functools

import jax
import jax.numpy as jnp
from jax import lax
from jax.experimental import pallas as pl
from jax.experimental.pallas import tpu as pltpu
from jax.sharding import PartitionSpec as P

HEADS = 16
HALF_WINDOW = 256
LANES = 128

smooth_sq = 0.01
alpha_fair = 0.95
NEG = -1e30
LOG2E = 1.4426950408889634

F32 = jnp.float32
BF16 = jnp.bfloat16
VMEM = pl.BlockSpec(memory_space=pltpu.VMEM)
SMEM = pl.BlockSpec(memory_space=pltpu.SMEM)
ANY = pl.BlockSpec(memory_space=pl.ANY)


def iota(shape, dim):
    return lax.broadcasted_iota(jnp.int32, shape, dim)


def normalize(x, scale):
    x32 = x.astype(F32)
    mean = jnp.mean(x32, axis=-1, keepdims=True)
    centred = x32 - mean
    var = jnp.mean(centred * centred, axis=-1, keepdims=True)
    return (centred * lax.rsqrt(var + 1e-05) * scale).astype(BF16)


def channel_scale(gain_ref, pert_ref):
    return gain_ref[...] * (1.0 + pert_ref[...].astype(F32))


def dead_flags(rows, live):
    return jnp.where((iota((rows, LANES), 0) >= live) & (iota((rows, LANES), 1) == 0), 1.0, 0.0).astype(BF16)


def attend_block(query, keys, values, flags, store, pairs):
    half = HALF_WINDOW
    row = iota((2 * half, half), 0) % half
    col = iota((2 * half, half), 1)
    near = jnp.where(col >= row, 0.0, NEG)
    far = jnp.where(col < row, 0.0, NEG)
    bias = jnp.where(iota((2 * half, LANES), 1) == 0, NEG, 0.0).astype(BF16)
    ones = jnp.ones((3 * half, LANES), BF16)
    lane = iota((half, LANES), 1)
    first = lane < LANES // 2
    for c in range(pairs):
        q = query(c)
        zero = jnp.zeros_like(q)
        both = jnp.concatenate([jnp.where(first, q, zero), jnp.where(first, zero, q)], axis=0)
        both = jnp.concatenate([both, bias], axis=1)
        k = jnp.concatenate([keys(c), flags], axis=1)
        s = lax.dot_general(both, k, (((1,), (1,)), ((), ())), preferred_element_type=F32)
        s = jnp.concatenate([s[:, :half] + near, s[:, half : 2 * half], s[:, 2 * half :] + far], axis=1)
        top = jnp.max(s, axis=1, keepdims=True)
        p = jnp.exp2((s - top) * LOG2E).astype(BF16)
        v = jnp.concatenate([values(c), ones], axis=1)
        o = jnp.dot(p, v, preferred_element_type=F32)
        num = jnp.where(first, o[:half, :LANES], o[half:, :LANES])
        den = jnp.where(first, o[:half, LANES:], o[half:, LANES:])
        store(c, (num / den).astype(BF16))


def decode(x, attended, w_proj, w_fields):
    updated = (x.astype(F32) + jnp.dot(attended, w_proj, preferred_element_type=F32)).astype(BF16)
    return lax.dot_general(w_fields, updated, (((0,), (1,)), ((), ())), preferred_element_type=F32)


def cols(c):
    return slice(c * LANES, (c + 1) * LANES)


def inner_kernel(counts, x_ref, pert, gain, w_qkv, w_proj, w_fields, out, q_edge, kv, normed, q_in, att):
    rows, width = x_ref.shape
    half = HALF_WINDOW
    own = counts[lax.axis_index("node")]
    scale = channel_scale(gain, pert)
    for b in range(rows // half):
        normed[b * half : (b + 1) * half, :] = normalize(x_ref[b * half : (b + 1) * half, :], scale)
    step = 256

    def project(j, _):
        at = pl.ds(pl.multiple_of(j * step, step), step)
        q = jnp.dot(normed[...], w_qkv[:, at], preferred_element_type=F32).astype(BF16)
        q = q * jnp.asarray((width // HEADS) ** -0.5, BF16)
        q_edge[:half, at] = q[:half]
        q_in[:, at] = q[half : rows - half]
        q_edge[half:, at] = q[rows - half :]
        return 0

    lax.fori_loop(0, width // step, project, 0)

    def project_kv(j, _):
        at = pl.ds(pl.multiple_of(j * step, step), step)
        src = pl.ds(pl.multiple_of(width + j * step, step), step)
        kv[:, at] = jnp.dot(normed[...], w_qkv[:, src], preferred_element_type=F32).astype(BF16)
        return 0

    lax.fori_loop(0, 2 * width // step, project_kv, 0)

    def block(b, _):
        start = pl.multiple_of(b * half, half)
        here = pl.ds(start, half)
        window = pl.ds(start, 3 * half)

        def store(c, value):
            att[:, cols(c)] = value

        attend_block(
            lambda c: q_in[here, cols(c)],
            lambda c: kv[window, cols(c)],
            lambda c: kv[window, slice(width + c * LANES, width + (c + 1) * LANES)],
            dead_flags(3 * half, own - start),
            store,
            width // LANES,
        )
        x = x_ref[pl.ds(pl.multiple_of(start + half, half), half), :]
        fields = decode(x, att[...], w_proj[...], w_fields[...])
        live = iota(fields.shape, 1) + start + half < own
        out[:, pl.ds(start, half)] = jnp.where(live, fields, 0.0).astype(BF16)
        return 0

    lax.fori_loop(0, rows // half - 2, block, 0)


def edge_kernel(counts, low, high, x_ref, pert, gain, w_qkv, w_proj, w_fields, q_edge, kv, out, normed, halo, att):
    rows, width = x_ref.shape
    half = HALF_WINDOW
    place = lax.axis_index("node")
    shards = counts.shape[0]
    own = counts[place]
    low_live = jnp.where(place > 0, counts[jnp.maximum(place - 1, 0)], 0)
    high_live = jnp.where(place < shards - 1, counts[jnp.minimum(place + 1, shards - 1)], 0)
    scale = channel_scale(gain, pert)
    normed[:half, :] = normalize(low[...], scale)
    normed[half:, :] = normalize(high[...], scale)
    step = 256

    def project_kv(j, _):
        at = pl.ds(pl.multiple_of(j * step, step), step)
        src = pl.ds(pl.multiple_of(width + j * step, step), step)
        halo[:, at] = jnp.dot(normed[...], w_qkv[:, src], preferred_element_type=F32).astype(BF16)
        return 0

    lax.fori_loop(0, 2 * width // step, project_kv, 0)

    def store(c, value):
        att[:, cols(c)] = value

    def vcols(c):
        return slice(width + c * LANES, width + (c + 1) * LANES)

    flags_low = jnp.concatenate([dead_flags(half, low_live - (rows - half)), dead_flags(2 * half, own)], axis=0)
    flags_high = jnp.concatenate(
        [dead_flags(2 * half, own - (rows - 2 * half)), dead_flags(half, high_live)], axis=0
    )
    tail = rows - 2 * half
    for side in range(2):
        if side == 0:
            q = lambda c: q_edge[:half, cols(c)]
            k = lambda c: jnp.concatenate([halo[:half, cols(c)], kv[: 2 * half, cols(c)]], axis=0)
            v = lambda c: jnp.concatenate([halo[:half, vcols(c)], kv[: 2 * half, vcols(c)]], axis=0)
            flags, start = flags_low, 0
        else:
            q = lambda c: q_edge[half:, cols(c)]
            k = lambda c: jnp.concatenate([kv[tail:, cols(c)], halo[half:, cols(c)]], axis=0)
            v = lambda c: jnp.concatenate([kv[tail:, vcols(c)], halo[half:, vcols(c)]], axis=0)
            flags, start = flags_high, rows - half
        attend_block(q, k, v, flags, store, width // LANES)
        fields = decode(x_ref[start : start + half, :], att[...], w_proj[...], w_fields[...])
        live = iota(fields.shape, 1) + start < own
        out[:, side * half : (side + 1) * half] = jnp.where(live, fields, 0.0).astype(BF16)


def score_values(mine, others, truth, live):
    total = 1 + len(others)
    eps = (1.0 - alpha_fair) / total
    mine = mine.astype(F32)
    others = [o.astype(F32) for o in others]

    def smooth(d):
        return jnp.sqrt(d * d + smooth_sq)

    d = mine - truth
    a = smooth(d)
    grad = d / a
    truth_sum = a
    for o in others:
        truth_sum = truth_sum + smooth(o - truth)
    pair_sum = jnp.zeros_like(a)
    pair_grad = jnp.zeros_like(a)
    for o in others:
        d = mine - o
        a = smooth(d)
        pair_sum = pair_sum + 2.0 * a
        pair_grad = pair_grad + d / a
    for i in range(len(others)):
        for j in range(i + 1, len(others)):
            pair_sum = pair_sum + 2.0 * smooth(others[i] - others[j])
    score = truth_sum * (1.0 / total) - (1.0 - eps) / (2.0 * total * (total - 1)) * pair_sum
    deriv = grad - (1.0 - eps) / (total - 1) * pair_grad
    return jnp.where(live, score, 0.0), jnp.where(live, deriv, 0.0)


def score_kernel(others, carried, place_of, counts, *refs):
    mine, rest, truth = refs[0], refs[1 : 1 + others], refs[1 + others]
    pred, score, deriv = refs[2 + others + carried :]
    width = mine.shape[1]
    own = counts[lax.axis_index("node")]
    start = place_of(pl.program_id(0)) * width
    live = iota(mine.shape, 1) + start < own
    pred[...] = mine[...]
    score[...], deriv[...] = score_values(mine[...], [r[...] for r in rest], truth[...], live)


def score_call(counts, mine, others, truth, carried, place_of, blocks):
    half = HALF_WINDOW
    fields, nodes = truth.shape
    part = pl.BlockSpec((fields, half), lambda i: (0, i))
    whole = pl.BlockSpec((fields, half), lambda i: (0, place_of(i)))
    shapes = [
        jax.ShapeDtypeStruct((fields, nodes), BF16),
        jax.ShapeDtypeStruct((fields, nodes), F32),
        jax.ShapeDtypeStruct((fields, nodes), F32),
    ]
    count = len(others)
    return pl.pallas_call(
        functools.partial(score_kernel, count, len(carried), place_of),
        grid=(blocks,),
        in_specs=[SMEM] + [part] * (1 + count) + [whole] + [ANY] * len(carried),
        out_specs=[whole] * 3,
        out_shape=shapes,
        input_output_aliases={3 + count + i: i for i in range(len(carried))},
        cost_estimate=pl.CostEstimate(
            flops=40 * fields * half * blocks, bytes_accessed=20 * fields * half * blocks, transcendentals=0
        ),
    )(counts, mine, *others, truth, *carried)


def on_device(hidden, pert, gain, w_qkv, w_proj, w_fields, truth, counts):
    _, rows, width = hidden.shape
    fields = w_fields.shape[1]
    half = HALF_WINDOW
    blocks = rows // half
    x = hidden[0]
    gain = gain.reshape(1, width)
    shards = lax.axis_size("node")
    members = lax.axis_size("ens")
    up = [(i, i + 1) for i in range(shards - 1)]
    down = [(t, s) for s, t in up]
    low = lax.ppermute(x[rows - half :], "node", up)
    high = lax.ppermute(x[:half], "node", down)

    inner = rows - 2 * half
    pred_in, q_edge, kv = pl.pallas_call(
        inner_kernel,
        in_specs=[SMEM, VMEM, VMEM, VMEM, VMEM, VMEM, VMEM],
        out_specs=[VMEM, VMEM, VMEM],
        out_shape=[
            jax.ShapeDtypeStruct((fields, inner), BF16),
            jax.ShapeDtypeStruct((2 * half, width), BF16),
            jax.ShapeDtypeStruct((rows, 2 * width), BF16),
        ],
        scratch_shapes=[
            pltpu.VMEM((rows, width), BF16),
            pltpu.VMEM((inner, width), BF16),
            pltpu.VMEM((half, width), BF16),
        ],
        cost_estimate=pl.CostEstimate(
            flops=2 * rows * width * 3 * width + 2 * inner * width * width + 12 * inner * width * half,
            bytes_accessed=10 * width * width,
            transcendentals=inner * HEADS * 3 * half,
        ),
        name="inner_blocks",
    )(counts, x, pert, gain, w_qkv, w_proj, w_fields)

    def exchange(part):
        return [
            lax.ppermute(part, "ens", [(i, (i + s) % members) for i in range(members)])
            for s in range(1, members)
        ]

    others_in = exchange(pred_in)
    pred_edge = pl.pallas_call(
        edge_kernel,
        in_specs=[SMEM] + [VMEM] * 10,
        out_specs=VMEM,
        out_shape=jax.ShapeDtypeStruct((fields, 2 * half), BF16),
        scratch_shapes=[
            pltpu.VMEM((2 * half, width), BF16),
            pltpu.VMEM((2 * half, 2 * width), BF16),
            pltpu.VMEM((half, width), BF16),
        ],
        cost_estimate=pl.CostEstimate(
            flops=2 * 2 * half * width * 3 * width + 12 * 2 * half * width * half,
            bytes_accessed=10 * width * width,
            transcendentals=2 * half * HEADS * 3 * half,
        ),
        name="edge_blocks",
    )(counts, low, high, x, pert, gain, w_qkv, w_proj, w_fields, q_edge, kv)
    others_edge = exchange(pred_edge)
    partial = score_call(counts, pred_in, others_in, truth, [], lambda i: i + 1, blocks - 2)
    pred, score, deriv = score_call(
        counts, pred_edge, others_edge, truth, partial, lambda i: i * (blocks - 1), 2
    )
    return pred[None], score, deriv[None]


def solution(mesh):
    return jax.shard_map(
        on_device,
        mesh=mesh,
        in_specs=(P("ens", "node", None), P("ens", None), P(), P(), P(), P(), P(None, "node"), P()),
        out_specs=(P("ens", None, "node"), P(None, "node"), P("ens", None, "node")),
        check_vma=False,
    )
```

```python
import functools

import jax
import jax.numpy as jnp
from jax import lax
from jax.experimental import pallas as pl
from jax.experimental.pallas import tpu as pltpu
from jax.sharding import PartitionSpec as P

HEADS = 16
HALF_WINDOW = 256
LANES = 128

smooth_sq = 0.01
alpha_fair = 0.95
NEG = -1e30
LOG2E = 1.4426950408889634

F32 = jnp.float32
BF16 = jnp.bfloat16
VMEM = pl.BlockSpec(memory_space=pltpu.VMEM)
SMEM = pl.BlockSpec(memory_space=pltpu.SMEM)
ANY = pl.BlockSpec(memory_space=pl.ANY)


def iota(shape, dim):
    return lax.broadcasted_iota(jnp.int32, shape, dim)


def normalize(x, scale):
    x32 = x.astype(F32)
    mean = jnp.mean(x32, axis=-1, keepdims=True)
    centred = x32 - mean
    var = jnp.mean(centred * centred, axis=-1, keepdims=True)
    return (centred * lax.rsqrt(var + 1e-05) * scale).astype(BF16)


def channel_scale(gain_ref, pert_ref):
    return gain_ref[...] * (1.0 + pert_ref[...].astype(F32))


def dead_flags(rows, live):
    return jnp.where((iota((rows, LANES), 0) >= live) & (iota((rows, LANES), 1) == 0), 1.0, 0.0).astype(BF16)


def attend_block(query, keys, values, flags, store, pairs):
    half = HALF_WINDOW
    row = iota((2 * half, half), 0) % half
    col = iota((2 * half, half), 1)
    near = jnp.where(col >= row, 0.0, NEG)
    far = jnp.where(col < row, 0.0, NEG)
    bias = jnp.where(iota((2 * half, LANES), 1) == 0, NEG, 0.0).astype(BF16)
    ones = jnp.ones((3 * half, LANES), BF16)
    lane = iota((half, LANES), 1)
    first = lane < LANES // 2
    for c in range(pairs):
        q = query(c)
        zero = jnp.zeros_like(q)
        both = jnp.concatenate([jnp.where(first, q, zero), jnp.where(first, zero, q)], axis=0)
        both = jnp.concatenate([both, bias], axis=1)
        k = jnp.concatenate([keys(c), flags], axis=1)
        s = lax.dot_general(both, k, (((1,), (1,)), ((), ())), preferred_element_type=F32)
        s = jnp.concatenate([s[:, :half] + near, s[:, half : 2 * half], s[:, 2 * half :] + far], axis=1)
        top = jnp.max(s, axis=1, keepdims=True)
        p = jnp.exp2((s - top) * LOG2E).astype(BF16)
        v = jnp.concatenate([values(c), ones], axis=1)
        o = jnp.dot(p, v, preferred_element_type=F32)
        num = jnp.where(first, o[:half, :LANES], o[half:, :LANES])
        den = jnp.where(first, o[:half, LANES:], o[half:, LANES:])
        store(c, (num / den).astype(BF16))


def decode(x, attended, w_proj, w_fields):
    updated = (x.astype(F32) + jnp.dot(attended, w_proj, preferred_element_type=F32)).astype(BF16)
    return lax.dot_general(w_fields, updated, (((1,), (1,)), ((), ())), preferred_element_type=F32)


def cols(c):
    return slice(c * LANES, (c + 1) * LANES)


def copies(pairs, sems, base=0):
    return [pltpu.make_async_copy(src, dst, sems.at[base + i]) for i, (src, dst) in enumerate(pairs)]


STEP = 256


def chunk(j, offset=0):
    return pl.ds(pl.multiple_of(offset + j * STEP, STEP), STEP)


def inner_kernel(
    counts, pert, gain, w_fields, x_hbm, w_qkv_hbm, w_proj_hbm,
    out, q_edge_hbm, kv_hbm,
    x, w_qkv, w_proj, normed, q_in, q_edge, kv, att, x_sem, w_sem, p_sem, q_sem, kv_sem,
):
    rows, width = x.shape
    half = HALF_WINDOW
    chunks = width // STEP
    own = counts[lax.axis_index("node")]

    def part(b):
        return slice(b * half, (b + 1) * half)

    x_in = copies([(x_hbm.at[part(b), :], x.at[part(b), :]) for b in range(rows // half)], x_sem)
    for c in x_in:
        c.start()

    def weight(j):
        return pltpu.make_async_copy(w_qkv_hbm.at[:, chunk(j)], w_qkv.at[:, chunk(j)], w_sem.at[j])

    for j in range(3 * chunks):
        weight(j).start()
    proj_in = pltpu.make_async_copy(w_proj_hbm, w_proj, p_sem)
    proj_in.start()
    scale = channel_scale(gain, pert)
    for b in range(rows // half):
        x_in[b].wait()
        normed[part(b), :] = normalize(x[part(b), :], scale)

    def project(j, _):
        weight(j).wait()
        q = jnp.dot(normed[...], w_qkv[:, chunk(j)], preferred_element_type=F32).astype(BF16)
        q = q * jnp.asarray((width // HEADS) ** -0.5, BF16)
        q_edge[:half, chunk(j)] = q[:half]
        q_in[:, chunk(j)] = q[half : rows - half]
        q_edge[half:, chunk(j)] = q[rows - half :]
        return 0

    lax.fori_loop(0, chunks, project, 0)
    q_out = pltpu.make_async_copy(q_edge, q_edge_hbm, q_sem)
    q_out.start()

    def kv_out(j):
        return pltpu.make_async_copy(kv.at[:, chunk(j)], kv_hbm.at[:, chunk(j)], kv_sem.at[j])

    def project_kv(j, _):
        weight(chunks + j).wait()
        w = w_qkv[:, chunk(j, width)]
        kv[:, chunk(j)] = jnp.dot(normed[...], w, preferred_element_type=F32).astype(BF16)
        kv_out(j).start()
        return 0

    lax.fori_loop(0, 2 * chunks, project_kv, 0)
    proj_in.wait()

    def block(b, _):
        start = pl.multiple_of(b * half, half)
        here = pl.ds(start, half)
        window = pl.ds(start, 3 * half)

        def store(c, value):
            att[:, cols(c)] = value

        attend_block(
            lambda c: q_in[here, cols(c)],
            lambda c: kv[window, cols(c)],
            lambda c: kv[window, slice(width + c * LANES, width + (c + 1) * LANES)],
            dead_flags(3 * half, own - start),
            store,
            width // LANES,
        )
        rest = x[pl.ds(pl.multiple_of(start + half, half), half), :]
        fields = decode(rest, att[...], w_proj[...], w_fields[...])
        live = iota(fields.shape, 1) + start + half < own
        out[:, pl.ds(start, half)] = jnp.where(live, fields, 0.0).astype(BF16)
        return 0

    lax.fori_loop(0, rows // half - 2, block, 0)
    q_out.wait()
    for j in range(2 * chunks):
        kv_out(j).wait()


def edge_kernel(
    counts, pert, gain, w_fields, low, high, x_hbm, w_qkv_hbm, w_proj_hbm, q_edge_hbm, kv_hbm,
    out,
    x, w_kv, w_proj, normed, halo, q_edge, kv, att, x_sem, w_sem, p_sem, q_sem, kv_sem,
):
    rows, width = kv_hbm.shape[0], w_proj.shape[0]
    half = HALF_WINDOW
    chunks = width // STEP
    tail = rows - 2 * half

    def weight(j):
        return pltpu.make_async_copy(w_qkv_hbm.at[:, chunk(j, width)], w_kv.at[:, chunk(j)], w_sem.at[j])

    for j in range(2 * chunks):
        weight(j).start()
    late = [
        pltpu.make_async_copy(q_edge_hbm, q_edge, q_sem),
        pltpu.make_async_copy(kv_hbm, kv, kv_sem),
        pltpu.make_async_copy(w_proj_hbm, w_proj, p_sem),
    ] + copies(
        [(x_hbm.at[:half, :], x.at[:half, :]), (x_hbm.at[rows - half :, :], x.at[half:, :])], x_sem
    )
    for c in late:
        c.start()
    place = lax.axis_index("node")
    shards = counts.shape[0]
    own = counts[place]
    low_live = jnp.where(place > 0, counts[jnp.maximum(place - 1, 0)], 0)
    high_live = jnp.where(place < shards - 1, counts[jnp.minimum(place + 1, shards - 1)], 0)
    scale = channel_scale(gain, pert)
    normed[:half, :] = normalize(low[...], scale)
    normed[half:, :] = normalize(high[...], scale)

    def project_kv(j, _):
        weight(j).wait()
        halo[:, chunk(j)] = jnp.dot(normed[...], w_kv[:, chunk(j)], preferred_element_type=F32).astype(BF16)
        return 0

    lax.fori_loop(0, 2 * chunks, project_kv, 0)
    for c in late:
        c.wait()

    def store(c, value):
        att[:, cols(c)] = value

    def vcols(c):
        return slice(width + c * LANES, width + (c + 1) * LANES)

    flags_low = jnp.concatenate([dead_flags(half, low_live - (rows - half)), dead_flags(2 * half, own)], axis=0)
    flags_high = jnp.concatenate([dead_flags(2 * half, own - tail), dead_flags(half, high_live)], axis=0)
    for side in range(2):
        if side == 0:
            q = lambda c: q_edge[:half, cols(c)]
            k = lambda c: jnp.concatenate([halo[:half, cols(c)], kv[: 2 * half, cols(c)]], axis=0)
            v = lambda c: jnp.concatenate([halo[:half, vcols(c)], kv[: 2 * half, vcols(c)]], axis=0)
            flags, start = flags_low, 0
        else:
            q = lambda c: q_edge[half:, cols(c)]
            k = lambda c: jnp.concatenate([kv[tail:, cols(c)], halo[half:, cols(c)]], axis=0)
            v = lambda c: jnp.concatenate([kv[tail:, vcols(c)], halo[half:, vcols(c)]], axis=0)
            flags, start = flags_high, rows - half
        attend_block(q, k, v, flags, store, width // LANES)
        rest = x[side * half : (side + 1) * half, :]
        fields = decode(rest, att[...], w_proj[...], w_fields[...])
        live = iota(fields.shape, 1) + start < own
        out[:, side * half : (side + 1) * half] = jnp.where(live, fields, 0.0).astype(BF16)


def score_values(mine, others, truth, live):
    total = 1 + len(others)
    eps = (1.0 - alpha_fair) / total
    mine = mine.astype(F32)
    others = [o.astype(F32) for o in others]

    def smooth(d):
        return jnp.sqrt(d * d + smooth_sq)

    d = mine - truth
    a = smooth(d)
    grad = d / a
    truth_sum = a
    for o in others:
        truth_sum = truth_sum + smooth(o - truth)
    pair_sum = jnp.zeros_like(a)
    pair_grad = jnp.zeros_like(a)
    for o in others:
        d = mine - o
        a = smooth(d)
        pair_sum = pair_sum + 2.0 * a
        pair_grad = pair_grad + d / a
    for i in range(len(others)):
        for j in range(i + 1, len(others)):
            pair_sum = pair_sum + 2.0 * smooth(others[i] - others[j])
    score = truth_sum * (1.0 / total) - (1.0 - eps) / (2.0 * total * (total - 1)) * pair_sum
    deriv = grad - (1.0 - eps) / (total - 1) * pair_grad
    return jnp.where(live, score, 0.0), jnp.where(live, deriv, 0.0)


def score_kernel(others, carried, place_of, counts, *refs):
    mine, rest, truth = refs[0], refs[1 : 1 + others], refs[1 + others]
    pred, score, deriv = refs[2 + others + carried :]
    width = mine.shape[1]
    own = counts[lax.axis_index("node")]
    start = place_of(pl.program_id(0)) * width
    live = iota(mine.shape, 1) + start < own
    pred[...] = mine[...]
    score[...], d = score_values(mine[...], [r[...] for r in rest], truth[...], live)
    deriv[...] = d[:, None, :]


def score_call(counts, mine, others, truth, carried, place_of, blocks):
    half = HALF_WINDOW
    fields, nodes = truth.shape
    part = pl.BlockSpec((fields, half), lambda i: (0, i))
    whole = pl.BlockSpec((fields, half), lambda i: (0, place_of(i)))
    flat = pl.BlockSpec((fields, 1, half), lambda i: (0, 0, place_of(i)))
    shapes = [
        jax.ShapeDtypeStruct((fields, nodes), BF16),
        jax.ShapeDtypeStruct((fields, nodes), F32),
        jax.ShapeDtypeStruct((fields, 1, nodes), F32),
    ]
    count = len(others)
    return pl.pallas_call(
        functools.partial(score_kernel, count, len(carried), place_of),
        grid=(blocks,),
        in_specs=[SMEM] + [part] * (1 + count) + [whole] + [ANY] * len(carried),
        out_specs=[whole, whole, flat],
        compiler_params=pltpu.CompilerParams(vmem_limit_bytes=8 << 20),
        out_shape=shapes,
        input_output_aliases={3 + count + i: i for i in range(len(carried))},
        cost_estimate=pl.CostEstimate(
            flops=40 * fields * half * blocks, bytes_accessed=20 * fields * half * blocks, transcendentals=0
        ),
    )(counts, mine, *others, truth, *carried)


def on_device(hidden, pert, gain, w_qkv, w_proj, w_fields, truth, counts):
    _, rows, width = hidden.shape
    fields = w_fields.shape[1]
    half = HALF_WINDOW
    chunks = width // STEP
    blocks = rows // half
    x = hidden[0]
    gain = gain.reshape(1, width)
    w_fields = w_fields.T
    shards = lax.axis_size("node")
    members = lax.axis_size("ens")
    up = [(i, i + 1) for i in range(shards - 1)]
    down = [(t, s) for s, t in up]
    low = lax.ppermute(x[rows - half :], "node", up)
    high = lax.ppermute(x[:half], "node", down)

    inner = rows - 2 * half
    dma = pltpu.SemaphoreType.DMA
    pred_in, q_edge, kv = pl.pallas_call(
        inner_kernel,
        in_specs=[SMEM, VMEM, VMEM, VMEM, ANY, ANY, ANY],
        out_specs=[VMEM, ANY, ANY],
        out_shape=[
            jax.ShapeDtypeStruct((fields, inner), BF16),
            jax.ShapeDtypeStruct((2 * half, width), BF16),
            jax.ShapeDtypeStruct((rows, 2 * width), BF16),
        ],
        scratch_shapes=[
            pltpu.VMEM((rows, width), BF16),
            pltpu.VMEM((width, 3 * width), BF16),
            pltpu.VMEM((width, width), BF16),
            pltpu.VMEM((rows, width), BF16),
            pltpu.VMEM((inner, width), BF16),
            pltpu.VMEM((2 * half, width), BF16),
            pltpu.VMEM((rows, 2 * width), BF16),
            pltpu.VMEM((half, width), BF16),
            dma((blocks,)),
            dma((3 * chunks,)),
            dma,
            dma,
            dma((2 * chunks,)),
        ],
        compiler_params=pltpu.CompilerParams(vmem_limit_bytes=48 << 20),
        cost_estimate=pl.CostEstimate(
            flops=2 * rows * width * 3 * width + 2 * inner * width * width + 12 * inner * width * half,
            bytes_accessed=10 * width * width,
            transcendentals=inner * HEADS * 3 * half,
        ),
        name="inner_blocks",
    )(counts, pert, gain, w_fields, x, w_qkv, w_proj)

    def exchange(part):
        return [
            lax.ppermute(part, "ens", [(i, (i + s) % members) for i in range(members)])
            for s in range(1, members)
        ]

    others_in = exchange(pred_in)
    pred_edge = pl.pallas_call(
        edge_kernel,
        in_specs=[SMEM] + [VMEM] * 5 + [ANY] * 5,
        out_specs=VMEM,
        out_shape=jax.ShapeDtypeStruct((fields, 2 * half), BF16),
        scratch_shapes=[
            pltpu.VMEM((2 * half, width), BF16),
            pltpu.VMEM((width, 2 * width), BF16),
            pltpu.VMEM((width, width), BF16),
            pltpu.VMEM((2 * half, width), BF16),
            pltpu.VMEM((2 * half, 2 * width), BF16),
            pltpu.VMEM((2 * half, width), BF16),
            pltpu.VMEM((rows, 2 * width), BF16),
            pltpu.VMEM((half, width), BF16),
            dma((2,)),
            dma((2 * chunks,)),
            dma,
            dma,
            dma,
        ],
        compiler_params=pltpu.CompilerParams(vmem_limit_bytes=48 << 20),
        cost_estimate=pl.CostEstimate(
            flops=2 * 2 * half * width * 3 * width + 12 * 2 * half * width * half,
            bytes_accessed=10 * width * width,
            transcendentals=2 * half * HEADS * 3 * half,
        ),
        name="edge_blocks",
    )(counts, pert, gain, w_fields, low, high, x, w_qkv, w_proj, q_edge, kv)
    others_edge = exchange(pred_edge)
    partial = score_call(counts, pred_in, others_in, truth, [], lambda i: i + 1, blocks - 2)
    pred, score, deriv = score_call(
        counts, pred_edge, others_edge, truth, partial, lambda i: i * (blocks - 1), 2
    )
    return pred[None], score, deriv.transpose(1, 0, 2)


def solution(mesh):
    return jax.shard_map(
        on_device,
        mesh=mesh,
        in_specs=(P("ens", "node", None), P("ens", None), P(), P(), P(), P(), P(None, "node"), P()),
        out_specs=(P("ens", None, "node"), P(None, "node"), P("ens", None, "node")),
        check_vma=False,
    )
```

```python
import functools

import jax
import jax.numpy as jnp
from jax import lax
from jax.experimental import pallas as pl
from jax.experimental.pallas import tpu as pltpu
from jax.sharding import PartitionSpec as P

HEADS = 16
HALF_WINDOW = 256
LANES = 128

smooth_sq = 0.01
alpha_fair = 0.95
NEG = -1e30
LOG2E = 1.4426950408889634
KERNEL_VMEM = 32 << 20

F32 = jnp.float32
BF16 = jnp.bfloat16
VMEM = pl.BlockSpec(memory_space=pltpu.VMEM)
SMEM = pl.BlockSpec(memory_space=pltpu.SMEM)
ANY = pl.BlockSpec(memory_space=pl.ANY)


def iota(shape, dim):
    return lax.broadcasted_iota(jnp.int32, shape, dim)


def normalize(x, scale):
    x32 = x.astype(F32)
    mean = jnp.mean(x32, axis=-1, keepdims=True)
    centred = x32 - mean
    var = jnp.mean(centred * centred, axis=-1, keepdims=True)
    return (centred * lax.rsqrt(var + 1e-05) * scale).astype(BF16)


def channel_scale(gain_ref, pert_ref):
    return gain_ref[...] * (1.0 + pert_ref[...].astype(F32))


def dead_flags(rows, live):
    return jnp.where((iota((rows, LANES), 0) >= live) & (iota((rows, LANES), 1) == 0), 1.0, 0.0).astype(BF16)


def attend_block(query, keys, values, flags, store, pairs):
    half = HALF_WINDOW
    row = iota((2 * half, half), 0) % half
    col = iota((2 * half, half), 1)
    near = jnp.where(col >= row, 0.0, NEG)
    far = jnp.where(col < row, 0.0, NEG)
    bias = jnp.where(iota((2 * half, LANES), 1) == 0, NEG, 0.0).astype(BF16)
    ones = jnp.ones((3 * half, LANES), BF16)
    lane = iota((half, LANES), 1)
    first = lane < LANES // 2
    for c in range(pairs):
        q = query(c)
        zero = jnp.zeros_like(q)
        both = jnp.concatenate([jnp.where(first, q, zero), jnp.where(first, zero, q)], axis=0)
        both = jnp.concatenate([both, bias], axis=1)
        k = jnp.concatenate([keys(c), flags], axis=1)
        s = lax.dot_general(both, k, (((1,), (1,)), ((), ())), preferred_element_type=F32)
        s = jnp.concatenate([s[:, :half] + near, s[:, half : 2 * half], s[:, 2 * half :] + far], axis=1)
        top = jnp.max(s, axis=1, keepdims=True)
        p = jnp.exp2((s - top) * LOG2E).astype(BF16)
        v = jnp.concatenate([values(c), ones], axis=1)
        o = jnp.dot(p, v, preferred_element_type=F32)
        num = jnp.where(first, o[:half, :LANES], o[half:, :LANES])
        den = jnp.where(first, o[:half, LANES:], o[half:, LANES:])
        store(c, (num / den).astype(BF16))


def decode(x, attended, w_proj, w_fields):
    updated = (x.astype(F32) + jnp.dot(attended, w_proj, preferred_element_type=F32)).astype(BF16)
    return lax.dot_general(w_fields, updated, (((1,), (1,)), ((), ())), preferred_element_type=F32)


def cols(c):
    return slice(c * LANES, (c + 1) * LANES)


def attend_side(q, kv, flags, att, q_at, k_at, width):
    def store(c, value):
        att[:, cols(c)] = value

    attend_block(
        lambda c: q[q_at, cols(c)],
        lambda c: kv[k_at, cols(c)],
        lambda c: kv[k_at, slice(width + c * LANES, width + (c + 1) * LANES)],
        flags,
        store,
        width // LANES,
    )


def inner_kernel(
    counts, x, pert_hbm, gain_hbm, w_fields_hbm, w_qkv_hbm, w_proj_hbm, out, q_edge, kv,
    pert, gain, w_fields, w_qkv, w_proj, normed, q_in, att, w_sem, s_sem,
):
    rows, width = x.shape
    scale_in = [
        pltpu.make_async_copy(pert_hbm, pert, s_sem.at[0]),
        pltpu.make_async_copy(gain_hbm, gain, s_sem.at[1]),
    ]
    w_in = [
        pltpu.make_async_copy(
            w_qkv_hbm.at[:, n * width : (n + 1) * width], w_qkv.at[:, n * width : (n + 1) * width], w_sem.at[n]
        )
        for n in range(3)
    ]
    late = [
        pltpu.make_async_copy(w_fields_hbm, w_fields, s_sem.at[2]),
        pltpu.make_async_copy(w_proj_hbm, w_proj, s_sem.at[3]),
    ]
    for c in scale_in + w_in + late:
        c.start()
    half = HALF_WINDOW
    blocks = rows // half
    own = counts[lax.axis_index("node")]
    head_scale = jnp.asarray((width // HEADS) ** -0.5, BF16)

    def part(b):
        return slice(b * half, (b + 1) * half)

    for c in scale_in:
        c.wait()
    scale = channel_scale(gain, pert)
    normed[part(0), :] = normalize(x[part(0), :], scale)
    for b in range(blocks):
        if b + 1 < blocks:
            normed[part(b + 1), :] = normalize(x[part(b + 1), :], scale)
        here = normed[part(b), :]
        for n in range(3):
            if b == 0:
                w_in[n].wait()
            res = jnp.dot(here, w_qkv[:, n * width : (n + 1) * width], preferred_element_type=F32).astype(BF16)
            if n > 0:
                kv[part(b), (n - 1) * width : n * width] = res
            elif b == 0:
                q_edge[:half, :] = res * head_scale
            elif b == blocks - 1:
                q_edge[half:, :] = res * head_scale
            else:
                q_in[part(b - 1), :] = res * head_scale

    for c in late:
        c.wait()

    def block(b, _):
        start = pl.multiple_of(b * half, half)
        attend_side(
            q_in, kv, dead_flags(3 * half, own - start), att, pl.ds(start, half), pl.ds(start, 3 * half), width
        )
        rest = x[pl.ds(pl.multiple_of(start + half, half), half), :]
        fields = decode(rest, att[...], w_proj[...], w_fields[...])
        live = iota(fields.shape, 1) + start + half < own
        out[:, pl.ds(start, half)] = jnp.where(live, fields, 0.0).astype(BF16)
        return 0

    lax.fori_loop(0, blocks - 2, block, 0)


def edge_kernel(
    counts, pert, gain, w_fields, first, second, x, w_qkv, w_proj, q_edge, kv_own, out, normed, kv, flags, att,
):
    rows, width = x.shape
    half = HALF_WINDOW
    place = lax.axis_index("node")
    shards = counts.shape[0]
    own = counts[place]
    low_live = jnp.where(place > 0, counts[jnp.maximum(place - 1, 0)], 0)
    high_live = jnp.where(place < shards - 1, counts[jnp.minimum(place + 1, shards - 1)], 0)
    scale = channel_scale(gain, pert)
    odd = lax.rem(place, 2)
    far = rows + half
    first_at = pl.ds(pl.multiple_of((1 - odd) * far, half), half)
    second_at = pl.ds(pl.multiple_of(odd * far, half), half)
    normed[:half, :] = normalize(first[...], scale)
    normed[half:, :] = normalize(second[...], scale)
    for n in range(2):
        w = w_qkv[:, (n + 1) * width : (n + 2) * width]
        at = slice(n * width, (n + 1) * width)
        kv[first_at, at] = jnp.dot(normed[:half, :], w, preferred_element_type=F32).astype(BF16)
        kv[second_at, at] = jnp.dot(normed[half:, :], w, preferred_element_type=F32).astype(BF16)
    kv[half:far, :] = kv_own[...]
    flags[:half, :] = dead_flags(half, low_live - (rows - half))
    flags[half:far, :] = dead_flags(rows, own)
    flags[far:, :] = dead_flags(half, high_live)

    def side(b, _):
        here = pl.ds(pl.multiple_of(b * half, half), half)
        start = pl.multiple_of(b * (rows - half), half)
        window = pl.ds(start, 3 * half)
        attend_side(q_edge, kv, flags[window, :], att, here, window, width)
        fields = decode(x[pl.ds(start, half), :], att[...], w_proj[...], w_fields[...])
        live = iota(fields.shape, 1) + start < own
        out[:, here] = jnp.where(live, fields, 0.0).astype(BF16)
        return 0

    lax.fori_loop(0, 2, side, 0)


def score_values(mine, others, truth, live):
    total = 1 + len(others)
    eps = (1.0 - alpha_fair) / total
    mine = mine.astype(F32)
    others = [o.astype(F32) for o in others]

    def smooth(d):
        return jnp.sqrt(d * d + smooth_sq)

    d = mine - truth
    a = smooth(d)
    grad = d / a
    truth_sum = a
    for o in others:
        truth_sum = truth_sum + smooth(o - truth)
    pair_sum = jnp.zeros_like(a)
    pair_grad = jnp.zeros_like(a)
    for o in others:
        d = mine - o
        a = smooth(d)
        pair_sum = pair_sum + 2.0 * a
        pair_grad = pair_grad + d / a
    for i in range(len(others)):
        for j in range(i + 1, len(others)):
            pair_sum = pair_sum + 2.0 * smooth(others[i] - others[j])
    score = truth_sum * (1.0 / total) - (1.0 - eps) / (2.0 * total * (total - 1)) * pair_sum
    deriv = grad - (1.0 - eps) / (total - 1) * pair_grad
    return jnp.where(live, score, 0.0), jnp.where(live, deriv, 0.0)


def score_kernel(others, carried, place_of, counts, *refs):
    mine, rest, truth = refs[0], refs[1 : 1 + others], refs[1 + others]
    pred, score, deriv = refs[2 + others + carried :]
    width = mine.shape[1]
    own = counts[lax.axis_index("node")]
    start = place_of(pl.program_id(0)) * width
    live = iota(mine.shape, 1) + start < own
    pred[...] = mine[...]
    score[...], d = score_values(mine[...], [r[...] for r in rest], truth[...], live)
    deriv[...] = d[:, None, :]


def score_call(counts, mine, others, truth, carried, place_of, blocks):
    half = HALF_WINDOW
    fields, nodes = truth.shape
    part = pl.BlockSpec((fields, half), lambda i: (0, i))
    whole = pl.BlockSpec((fields, half), lambda i: (0, place_of(i)))
    flat = pl.BlockSpec((fields, 1, half), lambda i: (0, 0, place_of(i)))
    shapes = [
        jax.ShapeDtypeStruct((fields, nodes), BF16),
        jax.ShapeDtypeStruct((fields, nodes), F32),
        jax.ShapeDtypeStruct((fields, 1, nodes), F32),
    ]
    count = len(others)
    return pl.pallas_call(
        functools.partial(score_kernel, count, len(carried), place_of),
        grid=(blocks,),
        in_specs=[SMEM] + [part] * (1 + count) + [whole] + [ANY] * len(carried),
        out_specs=[whole, whole, flat],
        compiler_params=pltpu.CompilerParams(vmem_limit_bytes=8 << 20),
        out_shape=shapes,
        input_output_aliases={3 + count + i: i for i in range(len(carried))},
        cost_estimate=pl.CostEstimate(
            flops=40 * fields * half * blocks, bytes_accessed=20 * fields * half * blocks, transcendentals=0
        ),
    )(counts, mine, *others, truth, *carried)


def neighbours(count, start):
    pairs = [(i, i + 1) for i in range(start, count - 1, 2)]
    return pairs + [(t, s) for s, t in pairs]


def on_device(hidden, pert, gain, w_qkv, w_proj, w_fields, truth, counts):
    _, rows, width = hidden.shape
    fields = w_fields.shape[1]
    half = HALF_WINDOW
    blocks = rows // half
    x = hidden[0]
    gain = gain.reshape(1, width)
    w_fields = w_fields.T
    shards = lax.axis_size("node")
    members = lax.axis_size("ens")
    odd = lax.axis_index("node") % 2
    facing = lax.dynamic_slice_in_dim(x, (1 - odd) * (rows - half), half, 0)
    first = lax.ppermute(facing, "node", neighbours(shards, 0))
    facing = lax.dynamic_slice_in_dim(x, odd * (rows - half), half, 0)
    second = lax.ppermute(facing, "node", neighbours(shards, 1))

    inner = rows - 2 * half
    pred_in, q_edge, kv = pl.pallas_call(
        inner_kernel,
        in_specs=[SMEM, VMEM] + [ANY] * 5,
        out_specs=[VMEM] * 3,
        out_shape=[
            jax.ShapeDtypeStruct((fields, inner), BF16),
            jax.ShapeDtypeStruct((2 * half, width), BF16),
            jax.ShapeDtypeStruct((rows, 2 * width), BF16),
        ],
        scratch_shapes=[
            pltpu.VMEM((1, width), BF16),
            pltpu.VMEM((1, width), F32),
            pltpu.VMEM((fields, width), BF16),
            pltpu.VMEM((width, 3 * width), BF16),
            pltpu.VMEM((width, width), BF16),
            pltpu.VMEM((rows, width), BF16),
            pltpu.VMEM((inner, width), BF16),
            pltpu.VMEM((half, width), BF16),
            pltpu.SemaphoreType.DMA((3,)),
            pltpu.SemaphoreType.DMA((4,)),
        ],
        compiler_params=pltpu.CompilerParams(vmem_limit_bytes=KERNEL_VMEM),
        cost_estimate=pl.CostEstimate(
            flops=2 * rows * width * 3 * width + 2 * inner * width * width + 12 * inner * width * half,
            bytes_accessed=10 * width * width,
            transcendentals=inner * HEADS * 3 * half,
        ),
        name="inner_blocks",
    )(counts, x, *[pltpu.with_memory_space_constraint(w, pltpu.HBM) for w in (pert, gain, w_fields, w_qkv, w_proj)])

    def exchange(part):
        return [
            lax.ppermute(part, "ens", [(i, (i + s) % members) for i in range(members)])
            for s in range(1, members)
        ]

    others_in = exchange(pred_in)
    pred_edge = pl.pallas_call(
        edge_kernel,
        in_specs=[SMEM] + [VMEM] * 10,
        out_specs=VMEM,
        out_shape=jax.ShapeDtypeStruct((fields, 2 * half), BF16),
        scratch_shapes=[
            pltpu.VMEM((2 * half, width), BF16),
            pltpu.VMEM((rows + 2 * half, 2 * width), BF16),
            pltpu.VMEM((rows + 2 * half, LANES), BF16),
            pltpu.VMEM((half, width), BF16),
        ],
        compiler_params=pltpu.CompilerParams(vmem_limit_bytes=KERNEL_VMEM),
        cost_estimate=pl.CostEstimate(
            flops=2 * 2 * half * width * 3 * width + 12 * 2 * half * width * half,
            bytes_accessed=10 * width * width,
            transcendentals=2 * half * HEADS * 3 * half,
        ),
        name="edge_blocks",
    )(counts, pert, gain, w_fields, first, second, x, w_qkv, w_proj, q_edge, kv)
    others_edge = exchange(pred_edge)
    partial = score_call(counts, pred_in, others_in, truth, [], lambda i: i + 1, blocks - 2)
    pred, score, deriv = score_call(
        counts, pred_edge, others_edge, truth, partial, lambda i: i * (blocks - 1), 2
    )
    return pred[None], score, deriv.transpose(1, 0, 2)


def solution(mesh):
    return jax.shard_map(
        on_device,
        mesh=mesh,
        in_specs=(P("ens", "node", None), P("ens", None), P(), P(), P(), P(), P(None, "node"), P()),
        out_specs=(P("ens", None, "node"), P(None, "node"), P("ens", None, "node")),
        check_vma=False,
    )
```

```python
import functools

import jax
import jax.numpy as jnp
from jax import lax
from jax.experimental import pallas as pl
from jax.experimental.pallas import tpu as pltpu
from jax.sharding import PartitionSpec as P

HEADS = 16
HALF_WINDOW = 256
LANES = 128

smooth_sq = 0.01
alpha_fair = 0.95
NEG = -1e30
LOG2E = 1.4426950408889634
KERNEL_VMEM = 32 << 20
FACING_FLOPS = 8_000_000_000

F32 = jnp.float32
BF16 = jnp.bfloat16
VMEM = pl.BlockSpec(memory_space=pltpu.VMEM)
SMEM = pl.BlockSpec(memory_space=pltpu.SMEM)
ANY = pl.BlockSpec(memory_space=pl.ANY)


def iota(shape, dim):
    return lax.broadcasted_iota(jnp.int32, shape, dim)


def normalize(x, scale):
    x32 = x.astype(F32)
    mean = jnp.mean(x32, axis=-1, keepdims=True)
    centred = x32 - mean
    var = jnp.mean(centred * centred, axis=-1, keepdims=True)
    return (centred * lax.rsqrt(var + 1e-05) * scale).astype(BF16)


def channel_scale(gain_ref, pert_ref):
    return gain_ref[...] * (1.0 + pert_ref[...].astype(F32))


def dead_flags(rows, live):
    return jnp.where((iota((rows, LANES), 0) >= live) & (iota((rows, LANES), 1) == 0), 1.0, 0.0).astype(BF16)


def attend_block(query, keys, values, flags, store, pairs):
    half = HALF_WINDOW
    row = iota((2 * half, half), 0) % half
    col = iota((2 * half, half), 1)
    near = jnp.where(col >= row, 0.0, NEG)
    far = jnp.where(col < row, 0.0, NEG)
    bias = jnp.where(iota((2 * half, LANES), 1) == 0, NEG, 0.0).astype(BF16)
    ones = jnp.ones((3 * half, LANES), BF16)
    lane = iota((half, LANES), 1)
    first = lane < LANES // 2
    for c in range(pairs):
        q = query(c)
        zero = jnp.zeros_like(q)
        both = jnp.concatenate([jnp.where(first, q, zero), jnp.where(first, zero, q)], axis=0)
        both = jnp.concatenate([both, bias], axis=1)
        k = jnp.concatenate([keys(c), flags], axis=1)
        s = lax.dot_general(both, k, (((1,), (1,)), ((), ())), preferred_element_type=F32)
        s = jnp.concatenate([s[:, :half] + near, s[:, half : 2 * half], s[:, 2 * half :] + far], axis=1)
        top = jnp.max(s, axis=1, keepdims=True)
        p = jnp.exp2((s - top) * LOG2E).astype(BF16)
        v = jnp.concatenate([values(c), ones], axis=1)
        o = jnp.dot(p, v, preferred_element_type=F32)
        num = jnp.where(first, o[:half, :LANES], o[half:, :LANES])
        den = jnp.where(first, o[:half, LANES:], o[half:, LANES:])
        store(c, (num / den).astype(BF16))


def decode(x, attended, w_proj, w_fields):
    updated = (x.astype(F32) + jnp.dot(attended, w_proj, preferred_element_type=F32)).astype(BF16)
    return lax.dot_general(w_fields, updated, (((1,), (1,)), ((), ())), preferred_element_type=F32)


def cols(c):
    return slice(c * LANES, (c + 1) * LANES)


def attend_side(q, kv, flags, att, q_at, k_at, width):
    def store(c, value):
        att[:, cols(c)] = value

    attend_block(
        lambda c: q[q_at, cols(c)],
        lambda c: kv[k_at, cols(c)],
        lambda c: kv[k_at, slice(width + c * LANES, width + (c + 1) * LANES)],
        flags,
        store,
        width // LANES,
    )


def facing_kernel(x, first, second, sem):
    rows = x.shape[0]
    half = first.shape[0]
    odd = lax.rem(lax.axis_index("node"), 2)
    at = [pl.multiple_of(o * (rows - half), half) for o in (1 - odd, odd)]
    moves = [
        pltpu.make_async_copy(x.at[pl.ds(a, half), :], out, sem.at[i])
        for i, (a, out) in enumerate(zip(at, (first, second)))
    ]
    for c in moves:
        c.start()
    for c in moves:
        c.wait()


def inner_kernel(counts, x, pert, gain, w_fields, w_qkv, w_proj, out, q_edge, kv, normed, q_in, att):
    rows, width = x.shape
    half = HALF_WINDOW
    blocks = rows // half
    own = counts[lax.axis_index("node")]
    head_scale = jnp.asarray((width // HEADS) ** -0.5, BF16)

    def part(b):
        return slice(b * half, (b + 1) * half)

    scale = channel_scale(gain, pert)
    normed[part(0), :] = normalize(x[part(0), :], scale)
    for b in range(blocks):
        if b + 1 < blocks:
            normed[part(b + 1), :] = normalize(x[part(b + 1), :], scale)
        here = normed[part(b), :]
        for n in range(3):
            res = jnp.dot(here, w_qkv[:, n * width : (n + 1) * width], preferred_element_type=F32).astype(BF16)
            if n > 0:
                kv[part(b), (n - 1) * width : n * width] = res
            elif b == 0:
                q_edge[:half, :] = res * head_scale
            elif b == blocks - 1:
                q_edge[half:, :] = res * head_scale
            else:
                q_in[part(b - 1), :] = res * head_scale

    def block(b, _):
        start = pl.multiple_of(b * half, half)
        attend_side(
            q_in, kv, dead_flags(3 * half, own - start), att, pl.ds(start, half), pl.ds(start, 3 * half), width
        )
        rest = x[pl.ds(pl.multiple_of(start + half, half), half), :]
        fields = decode(rest, att[...], w_proj[...], w_fields[...])
        live = iota(fields.shape, 1) + start + half < own
        out[:, pl.ds(start, half)] = jnp.where(live, fields, 0.0).astype(BF16)
        return 0

    lax.fori_loop(0, blocks - 2, block, 0)


def edge_kernel(
    counts, pert, gain, w_fields, first, second, x, w_qkv, w_proj, q_edge, kv_own, out, normed, kv, flags, att,
):
    rows, width = x.shape
    half = HALF_WINDOW
    place = lax.axis_index("node")
    shards = counts.shape[0]
    own = counts[place]
    low_live = jnp.where(place > 0, counts[jnp.maximum(place - 1, 0)], 0)
    high_live = jnp.where(place < shards - 1, counts[jnp.minimum(place + 1, shards - 1)], 0)
    scale = channel_scale(gain, pert)
    odd = lax.rem(place, 2)
    far = rows + half
    first_at = pl.ds(pl.multiple_of((1 - odd) * far, half), half)
    second_at = pl.ds(pl.multiple_of(odd * far, half), half)
    normed[:half, :] = normalize(first[...], scale)
    normed[half:, :] = normalize(second[...], scale)
    for n in range(2):
        w = w_qkv[:, (n + 1) * width : (n + 2) * width]
        at = slice(n * width, (n + 1) * width)
        kv[first_at, at] = jnp.dot(normed[:half, :], w, preferred_element_type=F32).astype(BF16)
        kv[second_at, at] = jnp.dot(normed[half:, :], w, preferred_element_type=F32).astype(BF16)
    kv[half:far, :] = kv_own[...]
    flags[:half, :] = dead_flags(half, low_live - (rows - half))
    flags[half:far, :] = dead_flags(rows, own)
    flags[far:, :] = dead_flags(half, high_live)

    def side(b, _):
        here = pl.ds(pl.multiple_of(b * half, half), half)
        start = pl.multiple_of(b * (rows - half), half)
        window = pl.ds(start, 3 * half)
        attend_side(q_edge, kv, flags[window, :], att, here, window, width)
        fields = decode(x[pl.ds(start, half), :], att[...], w_proj[...], w_fields[...])
        live = iota(fields.shape, 1) + start < own
        out[:, here] = jnp.where(live, fields, 0.0).astype(BF16)
        return 0

    lax.fori_loop(0, 2, side, 0)


def score_values(mine, others, truth, live):
    total = 1 + len(others)
    eps = (1.0 - alpha_fair) / total
    mine = mine.astype(F32)
    others = [o.astype(F32) for o in others]

    def smooth(d):
        return jnp.sqrt(d * d + smooth_sq)

    d = mine - truth
    a = smooth(d)
    grad = d / a
    truth_sum = a
    for o in others:
        truth_sum = truth_sum + smooth(o - truth)
    pair_sum = jnp.zeros_like(a)
    pair_grad = jnp.zeros_like(a)
    for o in others:
        d = mine - o
        a = smooth(d)
        pair_sum = pair_sum + 2.0 * a
        pair_grad = pair_grad + d / a
    for i in range(len(others)):
        for j in range(i + 1, len(others)):
            pair_sum = pair_sum + 2.0 * smooth(others[i] - others[j])
    score = truth_sum * (1.0 / total) - (1.0 - eps) / (2.0 * total * (total - 1)) * pair_sum
    deriv = grad - (1.0 - eps) / (total - 1) * pair_grad
    return jnp.where(live, score, 0.0), jnp.where(live, deriv, 0.0)


def score_kernel(others, carried, places, counts, *refs):
    mine, rest, truth = refs[0], refs[1 : 1 + others], refs[1 + others]
    pred, score, deriv = refs[2 + others + carried : 5 + others + carried]
    score_buf, deriv_buf, sem = refs[5 + others + carried :]
    half = HALF_WINDOW
    own = counts[lax.axis_index("node")]
    moves = []
    for i, place in enumerate(places):
        here, there = slice(i * half, (i + 1) * half), slice(place * half, (place + 1) * half)
        moves.append(pltpu.make_async_copy(mine.at[:, here], pred.at[:, there], sem.at[0, i]))
        moves[-1].start()
    for i, place in enumerate(places):
        here, there = slice(i * half, (i + 1) * half), slice(place * half, (place + 1) * half)
        f = mine[:, here]
        live = iota(f.shape, 1) + place * half < own
        score_buf[i], d = score_values(f, [r[:, here] for r in rest], truth[:, there], live)
        moves.append(pltpu.make_async_copy(score_buf.at[i], score.at[:, there], sem.at[1, i]))
        moves[-1].start()
        deriv_buf[i] = d[:, None, :]
        moves.append(pltpu.make_async_copy(deriv_buf.at[i], deriv.at[:, :, there], sem.at[2, i]))
        moves[-1].start()
    for c in moves:
        c.wait()


def score_call(counts, mine, others, truth, carried, places):
    half = HALF_WINDOW
    fields, nodes = truth.shape
    shapes = [
        jax.ShapeDtypeStruct((fields, nodes), BF16),
        jax.ShapeDtypeStruct((fields, nodes), F32),
        jax.ShapeDtypeStruct((fields, 1, nodes), F32),
    ]
    count = len(others)
    parts = len(places)
    return pl.pallas_call(
        functools.partial(score_kernel, count, len(carried), places),
        in_specs=[SMEM] + [VMEM] * (2 + count) + [ANY] * len(carried),
        out_specs=[ANY] * 3,
        out_shape=shapes,
        scratch_shapes=[
            pltpu.VMEM((parts, fields, half), F32),
            pltpu.VMEM((parts, fields, 1, half), F32),
            pltpu.SemaphoreType.DMA((3, parts)),
        ],
        compiler_params=pltpu.CompilerParams(vmem_limit_bytes=8 << 20),
        input_output_aliases={3 + count + i: i for i in range(len(carried))},
        cost_estimate=pl.CostEstimate(
            flops=40 * fields * half * parts, bytes_accessed=20 * fields * half * parts, transcendentals=0
        ),
        name="score",
    )(counts, mine, *others, truth, *carried)


def neighbours(count, start):
    pairs = [(i, i + 1) for i in range(start, count - 1, 2)]
    return pairs + [(t, s) for s, t in pairs]


def on_device(hidden, pert, gain, w_qkv, w_proj, w_fields, truth, counts):
    _, rows, width = hidden.shape
    fields = w_fields.shape[1]
    half = HALF_WINDOW
    blocks = rows // half
    x = hidden[0]
    gain = gain.reshape(1, width)
    w_fields = w_fields.T
    shards = lax.axis_size("node")
    members = lax.axis_size("ens")
    halves = pl.pallas_call(
        facing_kernel,
        in_specs=[ANY],
        out_specs=[VMEM] * 2,
        out_shape=[jax.ShapeDtypeStruct((half, width), BF16)] * 2,
        scratch_shapes=[pltpu.SemaphoreType.DMA((2,))],
        compiler_params=pltpu.CompilerParams(vmem_limit_bytes=4 << 20),
        cost_estimate=pl.CostEstimate(flops=FACING_FLOPS, bytes_accessed=4 * half * width, transcendentals=0),
        name="facing",
    )(pltpu.with_memory_space_constraint(x, pltpu.HBM))
    first = lax.ppermute(halves[0], "node", neighbours(shards, 0))
    second = lax.ppermute(halves[1], "node", neighbours(shards, 1))

    inner = rows - 2 * half
    pred_in, q_edge, kv = pl.pallas_call(
        inner_kernel,
        in_specs=[SMEM] + [VMEM] * 6,
        out_specs=[VMEM] * 3,
        out_shape=[
            jax.ShapeDtypeStruct((fields, inner), BF16),
            jax.ShapeDtypeStruct((2 * half, width), BF16),
            jax.ShapeDtypeStruct((rows, 2 * width), BF16),
        ],
        scratch_shapes=[
            pltpu.VMEM((rows, width), BF16),
            pltpu.VMEM((inner, width), BF16),
            pltpu.VMEM((half, width), BF16),
        ],
        compiler_params=pltpu.CompilerParams(vmem_limit_bytes=KERNEL_VMEM),
        cost_estimate=pl.CostEstimate(
            flops=2 * rows * width * 3 * width + 2 * inner * width * width + 12 * inner * width * half,
            bytes_accessed=10 * width * width,
            transcendentals=inner * HEADS * 3 * half,
        ),
        name="inner_blocks",
    )(counts, x, pert, gain, w_fields, w_qkv, w_proj)

    def exchange(part):
        return [
            lax.ppermute(part, "ens", [(i, (i + s) % members) for i in range(members)])
            for s in range(1, members)
        ]

    others_in = exchange(pred_in)
    pred_edge = pl.pallas_call(
        edge_kernel,
        in_specs=[SMEM] + [VMEM] * 10,
        out_specs=VMEM,
        out_shape=jax.ShapeDtypeStruct((fields, 2 * half), BF16),
        scratch_shapes=[
            pltpu.VMEM((2 * half, width), BF16),
            pltpu.VMEM((rows + 2 * half, 2 * width), BF16),
            pltpu.VMEM((rows + 2 * half, LANES), BF16),
            pltpu.VMEM((half, width), BF16),
        ],
        compiler_params=pltpu.CompilerParams(vmem_limit_bytes=KERNEL_VMEM),
        cost_estimate=pl.CostEstimate(
            flops=2 * 2 * half * width * 3 * width + 12 * 2 * half * width * half,
            bytes_accessed=10 * width * width,
            transcendentals=2 * half * HEADS * 3 * half,
        ),
        name="edge_blocks",
    )(counts, pert, gain, w_fields, first, second, x, w_qkv, w_proj, q_edge, kv)
    others_edge = exchange(pred_edge)
    partial = score_call(counts, pred_in, others_in, truth, [], list(range(1, blocks - 1)))
    pred, score, deriv = score_call(counts, pred_edge, others_edge, truth, partial, [0, blocks - 1])
    return pred[None], score, deriv.transpose(1, 0, 2)


def solution(mesh):
    return jax.shard_map(
        on_device,
        mesh=mesh,
        in_specs=(P("ens", "node", None), P("ens", None), P(), P(), P(), P(), P(None, "node"), P()),
        out_specs=(P("ens", None, "node"), P(None, "node"), P("ens", None, "node")),
        check_vma=False,
    )
```

```python
import functools

import jax
import jax.numpy as jnp
from jax import lax
from jax.experimental import pallas as pl
from jax.experimental.pallas import tpu as pltpu
from jax.sharding import PartitionSpec as P

HEADS = 16
HALF_WINDOW = 256
LANES = 128

smooth_sq = 0.01
alpha_fair = 0.95
NEG = -1e30
LOG2E = 1.4426950408889634
KERNEL_VMEM = 32 << 20
FACING_FLOPS = 8_000_000_000

F32 = jnp.float32
BF16 = jnp.bfloat16
VMEM = pl.BlockSpec(memory_space=pltpu.VMEM)
SMEM = pl.BlockSpec(memory_space=pltpu.SMEM)
ANY = pl.BlockSpec(memory_space=pl.ANY)


def iota(shape, dim):
    return lax.broadcasted_iota(jnp.int32, shape, dim)


def normalize(x, scale):
    x32 = x.astype(F32)
    mean = jnp.mean(x32, axis=-1, keepdims=True)
    centred = x32 - mean
    var = jnp.mean(centred * centred, axis=-1, keepdims=True)
    return (centred * lax.rsqrt(var + 1e-05) * scale).astype(BF16)


def channel_scale(gain_ref, pert_ref):
    return gain_ref[...] * (1.0 + pert_ref[...].astype(F32))


def dead_flags(rows, live):
    return jnp.where((iota((rows, LANES), 0) >= live) & (iota((rows, LANES), 1) == 0), 1.0, 0.0).astype(BF16)


def attend_blocks(blocks, pairs):
    half = HALF_WINDOW
    row = iota((2 * half, half), 0) % half
    col = iota((2 * half, half), 1)
    near = jnp.where(col >= row, 0.0, NEG)
    far = jnp.where(col < row, 0.0, NEG)
    bias = jnp.where(iota((2 * half, LANES), 1) == 0, NEG, 0.0).astype(BF16)
    ones = jnp.ones((3 * half, LANES), BF16)
    lane = iota((half, LANES), 1)
    first = lane < LANES // 2

    def scores(block, c):
        query, keys, _, flags, _, _ = block
        q = query(c)
        zero = jnp.zeros_like(q)
        both = jnp.concatenate([jnp.where(first, q, zero), jnp.where(first, zero, q)], axis=0)
        both = jnp.concatenate([both, bias], axis=1)
        k = jnp.concatenate([keys(c), flags], axis=1)
        s = lax.dot_general(both, k, (((1,), (1,)), ((), ())), preferred_element_type=F32)
        return jnp.concatenate([s[:, :half] + near, s[:, half : 2 * half], s[:, 2 * half :] + far], axis=1)

    steps = [(block, c) for block in blocks for c in range(pairs)]
    later = scores(*steps[0])
    for n, (block, c) in enumerate(steps):
        s = later
        if n + 1 < len(steps):
            later = scores(*steps[n + 1])
        _, _, values, _, store, finish = block
        top = jnp.max(s, axis=1, keepdims=True)
        p = jnp.exp2((s - top) * LOG2E).astype(BF16)
        v = jnp.concatenate([values(c), ones], axis=1)
        o = jnp.dot(p, v, preferred_element_type=F32)
        num = jnp.where(first, o[:half, :LANES], o[half:, :LANES])
        den = jnp.where(first, o[:half, LANES:], o[half:, LANES:])
        store(c, (num / den).astype(BF16))
        if c == pairs - 1:
            finish()


def decode(x, attended, w_proj, w_fields):
    updated = (x.astype(F32) + jnp.dot(attended, w_proj, preferred_element_type=F32)).astype(BF16)
    return lax.dot_general(w_fields, updated, (((1,), (1,)), ((), ())), preferred_element_type=F32)


def cols(c):
    return slice(c * LANES, (c + 1) * LANES)


def block_of(q, kv, flags, att, q_at, k_at, width, finish):
    def store(c, value):
        att[:, cols(c)] = value

    return (
        lambda c: q[q_at, cols(c)],
        lambda c: kv[k_at, cols(c)],
        lambda c: kv[k_at, slice(width + c * LANES, width + (c + 1) * LANES)],
        flags,
        store,
        finish,
    )


def facing_kernel(x, first, second, sem):
    rows = x.shape[0]
    half = first.shape[0]
    odd = lax.rem(lax.axis_index("node"), 2)
    at = [pl.multiple_of(o * (rows - half), half) for o in (1 - odd, odd)]
    moves = [
        pltpu.make_async_copy(x.at[pl.ds(a, half), :], out, sem.at[i])
        for i, (a, out) in enumerate(zip(at, (first, second)))
    ]
    for c in moves:
        c.start()
    for c in moves:
        c.wait()


def inner_kernel(counts, x, pert, gain, w_fields, w_qkv, w_proj, out, q_edge, kv, normed, q_in, att):
    rows, width = x.shape
    half = HALF_WINDOW
    blocks = rows // half
    own = counts[lax.axis_index("node")]
    head_scale = jnp.asarray((width // HEADS) ** -0.5, BF16)

    def part(b):
        return slice(b * half, (b + 1) * half)

    scale = channel_scale(gain, pert)
    normed[part(0), :] = normalize(x[part(0), :], scale)
    for b in range(blocks):
        here = normed[part(b), :]
        for n in range(3):
            res = jnp.dot(here, w_qkv[:, n * width : (n + 1) * width], preferred_element_type=F32).astype(BF16)
            if n > 0:
                kv[part(b), (n - 1) * width : n * width] = res
            elif b == 0:
                q_edge[:half, :] = res * head_scale
            elif b == blocks - 1:
                q_edge[half:, :] = res * head_scale
            else:
                q_in[part(b - 1), :] = res * head_scale
            if n == 0 and b + 1 < blocks:
                normed[part(b + 1), :] = normalize(x[part(b + 1), :], scale)

    def block(b):
        start = b * half

        def finish():
            fields = decode(x[part(b + 1), :], att[b % 2], w_proj[...], w_fields[...])
            live = iota(fields.shape, 1) + start + half < own
            out[:, part(b)] = jnp.where(live, fields, 0.0).astype(BF16)

        window = slice(start, start + 3 * half)
        return block_of(q_in, kv, dead_flags(3 * half, own - start), att.at[b % 2], part(b), window, width, finish)

    attend_blocks([block(b) for b in range(blocks - 2)], width // LANES)


def edge_kernel(
    side, counts, pert, gain, w_fields, first, second, x, w_qkv, w_proj, q_edge, kv, *rest,
):
    *done, out, normed, halo, att = rest
    rows, width = x.shape
    half = HALF_WINDOW
    place = lax.axis_index("node")
    shards = counts.shape[0]
    own = counts[place]
    odd = lax.rem(place, 2)
    scale = channel_scale(gain, pert)
    mine = jnp.where(odd == 1 - side, first[...].astype(F32), second[...].astype(F32))
    normed[...] = normalize(mine, scale)
    for n in range(2):
        at = slice(n * width, (n + 1) * width)
        w = w_qkv[:, (n + 1) * width : (n + 2) * width]
        halo[:, at] = jnp.dot(normed[...], w, preferred_element_type=F32).astype(BF16)
    if side == 0:
        near = slice(0, 2 * half)
        there = jnp.where(place > 0, counts[jnp.maximum(place - 1, 0)], 0) - (rows - half)
        flags = [dead_flags(half, there), dead_flags(2 * half, own)]
    else:
        near = slice(rows - 2 * half, rows)
        there = jnp.where(place < shards - 1, counts[jnp.minimum(place + 1, shards - 1)], 0)
        flags = [dead_flags(2 * half, own - (rows - 2 * half)), dead_flags(half, there)]
    start = side * (rows - half)
    here = slice(side * half, (side + 1) * half)

    def window(c):
        parts = [halo[:, cols(c)], kv[near, cols(c)]]
        return jnp.concatenate(parts if side == 0 else parts[::-1], axis=0)

    def store(c, value):
        att[:, cols(c)] = value

    def finish():
        fields = decode(x[start : start + half, :], att[...], w_proj[...], w_fields[...])
        live = iota(fields.shape, 1) + start < own
        out[:, :half] = jnp.where(live, fields, 0.0).astype(BF16)

    if done:
        out[:, half:] = done[0][...]
    attend_blocks(
        [
            (
                lambda c: q_edge[here, cols(c)],
                window,
                lambda c: window(c + width // LANES),
                jnp.concatenate(flags, axis=0),
                store,
                finish,
            )
        ],
        width // LANES,
    )


def score_values(mine, others, truth, live):
    total = 1 + len(others)
    eps = (1.0 - alpha_fair) / total
    mine = mine.astype(F32)
    others = [o.astype(F32) for o in others]

    def smooth(d):
        return jnp.sqrt(d * d + smooth_sq)

    d = mine - truth
    a = smooth(d)
    grad = d / a
    truth_sum = a
    for o in others:
        truth_sum = truth_sum + smooth(o - truth)
    pair_sum = jnp.zeros_like(a)
    pair_grad = jnp.zeros_like(a)
    for o in others:
        d = mine - o
        a = smooth(d)
        pair_sum = pair_sum + 2.0 * a
        pair_grad = pair_grad + d / a
    for i in range(len(others)):
        for j in range(i + 1, len(others)):
            pair_sum = pair_sum + 2.0 * smooth(others[i] - others[j])
    score = truth_sum * (1.0 / total) - (1.0 - eps) / (2.0 * total * (total - 1)) * pair_sum
    deriv = grad - (1.0 - eps) / (total - 1) * pair_grad
    return jnp.where(live, score, 0.0), jnp.where(live, deriv, 0.0)


def score_kernel(others, carried, places, counts, *refs):
    mine, rest, truth = refs[0], refs[1 : 1 + others], refs[1 + others]
    pred, score, deriv = refs[2 + others + carried : 5 + others + carried]
    score_buf, deriv_buf, sem = refs[5 + others + carried :]
    half = HALF_WINDOW
    own = counts[lax.axis_index("node")]
    moves = []
    for i, place in enumerate(places):
        here, there = slice(i * half, (i + 1) * half), slice(place * half, (place + 1) * half)
        moves.append(pltpu.make_async_copy(mine.at[:, here], pred.at[:, there], sem.at[0, i]))
        moves[-1].start()
    for i, place in enumerate(places):
        here, there = slice(i * half, (i + 1) * half), slice(place * half, (place + 1) * half)
        f = mine[:, here]
        live = iota(f.shape, 1) + place * half < own
        score_buf[i], d = score_values(f, [r[:, here] for r in rest], truth[:, there], live)
        moves.append(pltpu.make_async_copy(score_buf.at[i], score.at[:, there], sem.at[1, i]))
        moves[-1].start()
        deriv_buf[i] = d[:, None, :]
        moves.append(pltpu.make_async_copy(deriv_buf.at[i], deriv.at[:, :, there], sem.at[2, i]))
        moves[-1].start()
    for c in moves:
        c.wait()


def score_call(counts, mine, others, truth, carried, places):
    half = HALF_WINDOW
    fields, nodes = truth.shape
    shapes = [
        jax.ShapeDtypeStruct((fields, nodes), BF16),
        jax.ShapeDtypeStruct((fields, nodes), F32),
        jax.ShapeDtypeStruct((fields, 1, nodes), F32),
    ]
    count = len(others)
    parts = len(places)
    return pl.pallas_call(
        functools.partial(score_kernel, count, len(carried), places),
        in_specs=[SMEM] + [VMEM] * (2 + count) + [ANY] * len(carried),
        out_specs=[ANY] * 3,
        out_shape=shapes,
        scratch_shapes=[
            pltpu.VMEM((parts, fields, half), F32),
            pltpu.VMEM((parts, fields, 1, half), F32),
            pltpu.SemaphoreType.DMA((3, parts)),
        ],
        compiler_params=pltpu.CompilerParams(vmem_limit_bytes=8 << 20),
        input_output_aliases={3 + count + i: i for i in range(len(carried))},
        cost_estimate=pl.CostEstimate(
            flops=40 * fields * half * parts, bytes_accessed=20 * fields * half * parts, transcendentals=0
        ),
        name="score",
    )(counts, mine, *others, truth, *carried)


def neighbours(count, start):
    pairs = [(i, i + 1) for i in range(start, count - 1, 2)]
    return pairs + [(t, s) for s, t in pairs]


def on_device(hidden, pert, gain, w_qkv, w_proj, w_fields, truth, counts):
    _, rows, width = hidden.shape
    fields = w_fields.shape[1]
    half = HALF_WINDOW
    blocks = rows // half
    x = hidden[0]
    gain = gain.reshape(1, width)
    w_fields = w_fields.T
    shards = lax.axis_size("node")
    members = lax.axis_size("ens")
    halves = pl.pallas_call(
        facing_kernel,
        in_specs=[ANY],
        out_specs=[VMEM] * 2,
        out_shape=[jax.ShapeDtypeStruct((half, width), BF16)] * 2,
        scratch_shapes=[pltpu.SemaphoreType.DMA((2,))],
        compiler_params=pltpu.CompilerParams(vmem_limit_bytes=4 << 20),
        cost_estimate=pl.CostEstimate(flops=FACING_FLOPS, bytes_accessed=4 * half * width, transcendentals=0),
        name="facing",
    )(pltpu.with_memory_space_constraint(x, pltpu.HBM))
    first = lax.ppermute(halves[0], "node", neighbours(shards, 0))
    second = lax.ppermute(halves[1], "node", neighbours(shards, 1))

    inner = rows - 2 * half
    pred_in, q_edge, kv = pl.pallas_call(
        inner_kernel,
        in_specs=[SMEM] + [VMEM] * 6,
        out_specs=[VMEM] * 3,
        out_shape=[
            jax.ShapeDtypeStruct((fields, inner), BF16),
            jax.ShapeDtypeStruct((2 * half, width), BF16),
            jax.ShapeDtypeStruct((rows, 2 * width), BF16),
        ],
        scratch_shapes=[
            pltpu.VMEM((rows, width), BF16),
            pltpu.VMEM((inner, width), BF16),
            pltpu.VMEM((2, half, width), BF16),
        ],
        compiler_params=pltpu.CompilerParams(vmem_limit_bytes=KERNEL_VMEM),
        cost_estimate=pl.CostEstimate(
            flops=2 * rows * width * 3 * width + 2 * inner * width * width + 12 * inner * width * half,
            bytes_accessed=10 * width * width,
            transcendentals=inner * HEADS * 3 * half,
        ),
        name="inner_blocks",
    )(counts, x, pert, gain, w_fields, w_qkv, w_proj)

    def exchange(part):
        return [
            lax.ppermute(part, "ens", [(i, (i + s) % members) for i in range(members)])
            for s in range(1, members)
        ]

    def edge(side, *done):
        return pl.pallas_call(
            functools.partial(edge_kernel, side),
            in_specs=[SMEM] + [VMEM] * (10 + len(done)),
            out_specs=VMEM,
            out_shape=jax.ShapeDtypeStruct((fields, half + sum(d.shape[1] for d in done)), BF16),
            scratch_shapes=[
                pltpu.VMEM((half, width), BF16),
                pltpu.VMEM((half, 2 * width), BF16),
                pltpu.VMEM((half, width), BF16),
            ],
            compiler_params=pltpu.CompilerParams(vmem_limit_bytes=KERNEL_VMEM),
            cost_estimate=pl.CostEstimate(
                flops=2 * half * width * 3 * width + 12 * half * width * half,
                bytes_accessed=10 * width * width,
                transcendentals=half * HEADS * 3 * half,
            ),
            name="edge_block",
        )(counts, pert, gain, w_fields, first, second, x, w_qkv, w_proj, q_edge, kv, *done)

    pred_most = edge(0, pred_in)
    others_most = exchange(pred_most)
    pred_last = edge(1)
    others_last = exchange(pred_last)
    partial = score_call(counts, pred_most, others_most, truth, [], list(range(blocks - 1)))
    pred, score, deriv = score_call(counts, pred_last, others_last, truth, partial, [blocks - 1])
    return pred[None], score, deriv.transpose(1, 0, 2)


def solution(mesh):
    return jax.shard_map(
        on_device,
        mesh=mesh,
        in_specs=(P("ens", "node", None), P("ens", None), P(), P(), P(), P(), P(None, "node"), P()),
        out_specs=(P("ens", None, "node"), P(None, "node"), P("ens", None, "node")),
        check_vma=False,
    )
```

```python
import functools

import jax
import jax.numpy as jnp
from jax import lax
from jax.experimental import pallas as pl
from jax.experimental.pallas import tpu as pltpu
from jax.sharding import PartitionSpec as P

HEADS = 16
HALF_WINDOW = 256
LANES = 128

smooth_sq = 0.01
alpha_fair = 0.95
NEG = -1e30
LOG2E = 1.4426950408889634
KERNEL_VMEM = 32 << 20
FACING_FLOPS = 8_000_000_000

F32 = jnp.float32
BF16 = jnp.bfloat16
VMEM = pl.BlockSpec(memory_space=pltpu.VMEM)
ANY = pl.BlockSpec(memory_space=pl.ANY)


def iota(shape, dim):
    return lax.broadcasted_iota(jnp.int32, shape, dim)


def normalize(x, scale):
    x32 = x.astype(F32)
    mean = jnp.mean(x32, axis=-1, keepdims=True)
    centred = x32 - mean
    var = jnp.mean(centred * centred, axis=-1, keepdims=True)
    return (centred * lax.rsqrt(var + 1e-05) * scale).astype(BF16)


def channel_scale(gain_ref, pert_ref):
    return gain_ref[...] * (1.0 + pert_ref[...].astype(F32))


def dead_flags(rows, live):
    return jnp.where((iota((rows, LANES), 0) >= live) & (iota((rows, LANES), 1) == 0), 1.0, 0.0).astype(BF16)


def attend_blocks(blocks, pairs):
    half = HALF_WINDOW
    sub = half // 2
    row = iota((sub, sub), 0)
    col = iota((sub, sub), 1)
    near = jnp.where(col >= row, 0.0, NEG)
    far = jnp.where(col < row, 0.0, NEG)
    bias = jnp.where(iota((2 * half, LANES), 1) == 0, NEG, 0.0).astype(BF16)
    ones = jnp.ones((3 * half, LANES), BF16)
    outside = jnp.zeros((sub, sub), BF16)
    lane = iota((half, LANES), 1)
    first = lane < LANES // 2

    def scores(block, c):
        query, keys, _, flags, _, _ = block
        q = query(c)
        zero = jnp.zeros_like(q)
        both = jnp.concatenate([jnp.where(first, q, zero), jnp.where(first, zero, q)], axis=0)
        both = jnp.concatenate([both, bias], axis=1)
        k = jnp.concatenate([keys(c), flags], axis=1)
        return lax.dot_general(both, k, (((1,), (1,)), ((), ())), preferred_element_type=F32)

    def weights(s):
        groups = []
        for g in range(4):
            t = s[g * sub : (g + 1) * sub, (g % 2) * sub : (g % 2) * sub + 5 * sub]
            t = jnp.concatenate([t[:, :sub] + near, t[:, sub : 4 * sub], t[:, 4 * sub :] + far], axis=1)
            top = jnp.max(t, axis=1, keepdims=True)
            p = jnp.exp2((t - top) * LOG2E).astype(BF16)
            groups.append(jnp.concatenate([p, outside] if g % 2 == 0 else [outside, p], axis=1))
        return jnp.concatenate(groups, axis=0)

    steps = [(block, c) for block in blocks for c in range(pairs)]
    later = scores(*steps[0])
    for n, (block, c) in enumerate(steps):
        s = later
        if n + 1 < len(steps):
            later = scores(*steps[n + 1])
        _, _, values, _, store, finish = block
        v = jnp.concatenate([values(c), ones], axis=1)
        o = jnp.dot(weights(s), v, preferred_element_type=F32)
        num = jnp.where(first, o[:half, :LANES], o[half:, :LANES])
        den = jnp.where(first, o[:half, LANES:], o[half:, LANES:])
        store(c, (num / den).astype(BF16))
        if c == pairs - 1:
            finish()


def decode(x, attended, w_proj, w_fields):
    updated = (x.astype(F32) + jnp.dot(attended, w_proj, preferred_element_type=F32)).astype(BF16)
    return lax.dot_general(w_fields, updated, (((1,), (1,)), ((), ())), preferred_element_type=F32)


def cols(c):
    return slice(c * LANES, (c + 1) * LANES)


def block_of(q, kv, flags, att, q_at, k_at, width, finish):
    def store(c, value):
        att[:, cols(c)] = value

    return (
        lambda c: q[q_at, cols(c)],
        lambda c: kv[k_at, cols(c)],
        lambda c: kv[k_at, slice(width + c * LANES, width + (c + 1) * LANES)],
        flags,
        store,
        finish,
    )


def facing_kernel(x, first, second, sem):
    rows = x.shape[0]
    half = first.shape[0]
    odd = lax.rem(lax.axis_index("node"), 2)
    at = [pl.multiple_of(o * (rows - half), half) for o in (1 - odd, odd)]
    moves = [
        pltpu.make_async_copy(x.at[pl.ds(a, half), :], out, sem.at[i])
        for i, (a, out) in enumerate(zip(at, (first, second)))
    ]
    for c in moves:
        c.start()
    for c in moves:
        c.wait()


def inner_kernel(
    counts, x, pert, gain, w_fields, w_qkv, w_proj, out, q_edge, kv, flags, alive, normed, q_in, att,
):
    rows, width = x.shape
    half = HALF_WINDOW
    blocks = rows // half
    place = lax.axis_index("node")
    shard = iota(counts.shape, 1)

    def count(at):
        return jnp.sum(jnp.where(shard == at, counts[...], 0), axis=1, keepdims=True)

    own, low_live, high_live = count(place), count(place - 1), count(place + 1)
    flags[:half, :] = dead_flags(half, low_live - (rows - half))
    flags[half : half + rows, :] = dead_flags(rows, own)
    flags[half + rows :, :] = dead_flags(half, high_live)
    alive[...] = jnp.where(iota(alive.shape, 1) < own, 1.0, 0.0)
    head_scale = jnp.asarray((width // HEADS) ** -0.5, BF16)

    def part(b):
        return slice(b * half, (b + 1) * half)

    scale = channel_scale(gain, pert)
    normed[part(0), :] = normalize(x[part(0), :], scale)
    for b in range(blocks):
        here = normed[part(b), :]
        for n in range(3):
            res = jnp.dot(here, w_qkv[:, n * width : (n + 1) * width], preferred_element_type=F32).astype(BF16)
            if n > 0:
                kv[part(b), (n - 1) * width : n * width] = res
            elif b == 0:
                q_edge[:half, :] = res * head_scale
            elif b == blocks - 1:
                q_edge[half:, :] = res * head_scale
            else:
                q_in[part(b - 1), :] = res * head_scale
            if n == 0 and b + 1 < blocks:
                normed[part(b + 1), :] = normalize(x[part(b + 1), :], scale)

    def block(b):
        start = b * half

        def finish():
            fields = decode(x[part(b + 1), :], att[b % 2], w_proj[...], w_fields[...])
            live = iota(fields.shape, 1) + start + half < own
            out[:, part(b)] = jnp.where(live, fields, 0.0).astype(BF16)

        window = slice(start, start + 3 * half)
        return block_of(q_in, kv, dead_flags(3 * half, own - start), att.at[b % 2], part(b), window, width, finish)

    attend_blocks([block(b) for b in range(blocks - 2)], width // LANES)


def edge_kernel(
    side, alive, flags, w_fields, x, w_proj, q_edge, kv, *refs,
):
    rows, width = x.shape
    half = HALF_WINDOW
    if side == 0:
        pert, gain, first, second, w_qkv, done, out, halo_high, normed, halo, att = refs
        odd = lax.rem(lax.axis_index("node"), 2)
        scale = channel_scale(gain, pert)
        low = jnp.where(odd == 1, first[...].astype(F32), second[...].astype(F32))
        normed[:half, :] = normalize(low, scale)
        for h, target in enumerate((halo, halo_high)):
            for n in range(2):
                at = slice(n * width, (n + 1) * width)
                w = w_qkv[:, (n + 1) * width : (n + 2) * width]
                rows_in = normed[h * half : (h + 1) * half, :]
                target[:, at] = jnp.dot(rows_in, w, preferred_element_type=F32).astype(BF16)
                if h == 0 and n == 0:
                    high = jnp.where(odd == 1, second[...].astype(F32), first[...].astype(F32))
                    normed[half:, :] = normalize(high, scale)
        near = slice(0, 2 * half)
        out[:, half:] = done[...]
    else:
        halo, out, att = refs
        near = slice(rows - 2 * half, rows)
    start = side * (rows - half)
    here = slice(side * half, (side + 1) * half)

    def window(c):
        parts = [halo[:, cols(c)], kv[near, cols(c)]]
        return jnp.concatenate(parts if side == 0 else parts[::-1], axis=0)

    def store(c, value):
        att[:, cols(c)] = value

    def finish():
        fields = decode(x[start : start + half, :], att[...], w_proj[...], w_fields[...])
        out[:, :half] = jnp.where(alive[:, start : start + half] > 0.0, fields, 0.0).astype(BF16)

    attend_blocks(
        [
            (
                lambda c: q_edge[here, cols(c)],
                window,
                lambda c: window(c + width // LANES),
                flags[start : start + 3 * half, :],
                store,
                finish,
            )
        ],
        width // LANES,
    )


def score_values(mine, others, truth, live):
    total = 1 + len(others)
    eps = (1.0 - alpha_fair) / total
    mine = mine.astype(F32)
    others = [o.astype(F32) for o in others]

    def smooth(d):
        return jnp.sqrt(d * d + smooth_sq)

    d = mine - truth
    a = smooth(d)
    grad = d / a
    truth_sum = a
    for o in others:
        truth_sum = truth_sum + smooth(o - truth)
    pair_sum = jnp.zeros_like(a)
    pair_grad = jnp.zeros_like(a)
    for o in others:
        d = mine - o
        a = smooth(d)
        pair_sum = pair_sum + 2.0 * a
        pair_grad = pair_grad + d / a
    for i in range(len(others)):
        for j in range(i + 1, len(others)):
            pair_sum = pair_sum + 2.0 * smooth(others[i] - others[j])
    score = truth_sum * (1.0 / total) - (1.0 - eps) / (2.0 * total * (total - 1)) * pair_sum
    deriv = grad - (1.0 - eps) / (total - 1) * pair_grad
    return jnp.where(live, score, 0.0), jnp.where(live, deriv, 0.0)


def score_kernel(others, carried, places, alive, *refs):
    mine, rest, truth = refs[0], refs[1 : 1 + others], refs[1 + others]
    pred, score, deriv = refs[2 + others + carried : 5 + others + carried]
    score_buf, deriv_buf, sem = refs[5 + others + carried :]
    half = HALF_WINDOW
    moves = []
    for i, place in enumerate(places):
        here, there = slice(i * half, (i + 1) * half), slice(place * half, (place + 1) * half)
        moves.append(pltpu.make_async_copy(mine.at[:, here], pred.at[:, there], sem.at[0, i]))
        moves[-1].start()
    for i, place in enumerate(places):
        here, there = slice(i * half, (i + 1) * half), slice(place * half, (place + 1) * half)
        f = mine[:, here]
        live = alive[:, there] > 0.0
        score_buf[i], d = score_values(f, [r[:, here] for r in rest], truth[:, there], live)
        moves.append(pltpu.make_async_copy(score_buf.at[i], score.at[:, there], sem.at[1, i]))
        moves[-1].start()
        deriv_buf[i] = d[:, None, :]
        moves.append(pltpu.make_async_copy(deriv_buf.at[i], deriv.at[:, :, there], sem.at[2, i]))
        moves[-1].start()
    for c in moves:
        c.wait()


def score_call(alive, mine, others, truth, carried, places):
    half = HALF_WINDOW
    fields, nodes = truth.shape
    shapes = [
        jax.ShapeDtypeStruct((fields, nodes), BF16),
        jax.ShapeDtypeStruct((fields, nodes), F32),
        jax.ShapeDtypeStruct((fields, 1, nodes), F32),
    ]
    count = len(others)
    parts = len(places)
    return pl.pallas_call(
        functools.partial(score_kernel, count, len(carried), places),
        in_specs=[VMEM] * (3 + count) + [ANY] * len(carried),
        out_specs=[ANY] * 3,
        out_shape=shapes,
        scratch_shapes=[
            pltpu.VMEM((parts, fields, half), F32),
            pltpu.VMEM((parts, fields, 1, half), F32),
            pltpu.SemaphoreType.DMA((3, parts)),
        ],
        compiler_params=pltpu.CompilerParams(vmem_limit_bytes=8 << 20),
        input_output_aliases={3 + count + i: i for i in range(len(carried))},
        cost_estimate=pl.CostEstimate(
            flops=40 * fields * half * parts, bytes_accessed=20 * fields * half * parts, transcendentals=0
        ),
        name="score",
    )(alive, mine, *others, truth, *carried)


def neighbours(count, start):
    pairs = [(i, i + 1) for i in range(start, count - 1, 2)]
    return pairs + [(t, s) for s, t in pairs]


def on_device(hidden, pert, gain, w_qkv, w_proj, w_fields, truth, counts):
    _, rows, width = hidden.shape
    fields = w_fields.shape[1]
    half = HALF_WINDOW
    blocks = rows // half
    x = hidden[0]
    gain = gain.reshape(1, width)
    w_fields = w_fields.T
    shards = lax.axis_size("node")
    members = lax.axis_size("ens")
    halves = pl.pallas_call(
        facing_kernel,
        in_specs=[ANY],
        out_specs=[VMEM] * 2,
        out_shape=[jax.ShapeDtypeStruct((half, width), BF16)] * 2,
        scratch_shapes=[pltpu.SemaphoreType.DMA((2,))],
        compiler_params=pltpu.CompilerParams(vmem_limit_bytes=4 << 20),
        cost_estimate=pl.CostEstimate(flops=FACING_FLOPS, bytes_accessed=4 * half * width, transcendentals=0),
        name="facing",
    )(pltpu.with_memory_space_constraint(x, pltpu.HBM))
    first = lax.ppermute(halves[0], "node", neighbours(shards, 0))
    second = lax.ppermute(halves[1], "node", neighbours(shards, 1))

    inner = rows - 2 * half
    pred_in, q_edge, kv, flags, alive = pl.pallas_call(
        inner_kernel,
        in_specs=[VMEM] * 7,
        out_specs=[VMEM] * 5,
        out_shape=[
            jax.ShapeDtypeStruct((fields, inner), BF16),
            jax.ShapeDtypeStruct((2 * half, width), BF16),
            jax.ShapeDtypeStruct((rows, 2 * width), BF16),
            jax.ShapeDtypeStruct((rows + 2 * half, LANES), BF16),
            jax.ShapeDtypeStruct((1, rows), F32),
        ],
        scratch_shapes=[
            pltpu.VMEM((rows, width), BF16),
            pltpu.VMEM((inner, width), BF16),
            pltpu.VMEM((2, half, width), BF16),
        ],
        compiler_params=pltpu.CompilerParams(vmem_limit_bytes=KERNEL_VMEM),
        cost_estimate=pl.CostEstimate(
            flops=2 * rows * width * 3 * width + 2 * inner * width * width + 12 * inner * width * half,
            bytes_accessed=10 * width * width,
            transcendentals=inner * HEADS * 3 * half,
        ),
        name="inner_blocks",
    )(counts.reshape(1, -1), x, pert, gain, w_fields, w_qkv, w_proj)

    def exchange(part):
        return [
            lax.ppermute(part, "ens", [(i, (i + s) % members) for i in range(members)])
            for s in range(1, members)
        ]

    def edge(side, out_shape, scratch, flops, *extra):
        return pl.pallas_call(
            functools.partial(edge_kernel, side),
            in_specs=[VMEM] * (7 + len(extra)),
            out_specs=[VMEM] * len(out_shape),
            out_shape=[jax.ShapeDtypeStruct(shape, BF16) for shape in out_shape],
            scratch_shapes=[pltpu.VMEM(shape, BF16) for shape in scratch],
            compiler_params=pltpu.CompilerParams(vmem_limit_bytes=KERNEL_VMEM),
            cost_estimate=pl.CostEstimate(
                flops=flops + 12 * half * width * half,
                bytes_accessed=10 * width * width,
                transcendentals=half * HEADS * 3 * half,
            ),
            name="edge_block",
        )(alive, flags, w_fields, x, w_proj, q_edge, kv, *extra)

    pred_most, halo_high = edge(
        0,
        [(fields, rows - half), (half, 2 * width)],
        [(2 * half, width), (half, 2 * width), (half, width)],
        10 * half * width * width,
        pert, gain, first, second, w_qkv, pred_in,
    )
    others_most = exchange(pred_most)
    (pred_last,) = edge(1, [(fields, half)], [(half, width)], 2 * half * width * width, halo_high)
    others_last = exchange(pred_last)
    partial = score_call(alive, pred_most, others_most, truth, [], list(range(blocks - 1)))
    pred, score, deriv = score_call(alive, pred_last, others_last, truth, partial, [blocks - 1])
    return pred[None], score, deriv.transpose(1, 0, 2)


def solution(mesh):
    return jax.shard_map(
        on_device,
        mesh=mesh,
        in_specs=(P("ens", "node", None), P("ens", None), P(), P(), P(), P(), P(None, "node"), P()),
        out_specs=(P("ens", None, "node"), P(None, "node"), P("ens", None, "node")),
        check_vma=False,
    )
```

```python
import functools

import jax
import jax.numpy as jnp
from jax import lax
from jax.experimental import pallas as pl
from jax.experimental.pallas import tpu as pltpu
from jax.sharding import PartitionSpec as P

HEADS = 16
HALF_WINDOW = 256
LANES = 128

smooth_sq = 0.01
alpha_fair = 0.95
NEG = -1e30
LOG2E = 1.4426950408889634
KERNEL_VMEM = 32 << 20
FACING_FLOPS = 8_000_000_000

F32 = jnp.float32
BF16 = jnp.bfloat16
VMEM = pl.BlockSpec(memory_space=pltpu.VMEM)
ANY = pl.BlockSpec(memory_space=pl.ANY)


def iota(shape, dim):
    return lax.broadcasted_iota(jnp.int32, shape, dim)


def normalize(x, scale):
    x32 = x.astype(F32)
    mean = jnp.mean(x32, axis=-1, keepdims=True)
    centred = x32 - mean
    var = jnp.mean(centred * centred, axis=-1, keepdims=True)
    return (centred * lax.rsqrt(var + 1e-05) * scale).astype(BF16)


def channel_scale(gain_ref, pert_ref):
    return gain_ref[...] * (1.0 + pert_ref[...].astype(F32))


def dead_flags(rows, live):
    return jnp.where((iota((rows, LANES), 0) >= live) & (iota((rows, LANES), 1) == 0), 1.0, 0.0).astype(BF16)


def attend_blocks(blocks, pairs):
    half = HALF_WINDOW
    sub = half // 2
    row = iota((sub, sub), 0)
    col = iota((sub, sub), 1)
    near = jnp.where(col >= row, 0.0, NEG)
    far = jnp.where(col < row, 0.0, NEG)
    bias = jnp.where(iota((2 * half, LANES), 1) == 0, NEG, 0.0).astype(BF16)
    ones = jnp.ones((3 * half, LANES), BF16)
    outside = jnp.zeros((sub, sub), BF16)
    lane = iota((half, LANES), 1)
    first = lane < LANES // 2

    def scores(block, c):
        query, keys, _, flags, _, _ = block
        q = query(c)
        zero = jnp.zeros_like(q)
        both = jnp.concatenate([jnp.where(first, q, zero), jnp.where(first, zero, q)], axis=0)
        both = jnp.concatenate([both, bias], axis=1)
        k = jnp.concatenate([keys(c), flags], axis=1)
        return lax.dot_general(both, k, (((1,), (1,)), ((), ())), preferred_element_type=F32)

    def weights(s):
        groups = []
        for g in range(4):
            t = s[g * sub : (g + 1) * sub, (g % 2) * sub : (g % 2) * sub + 5 * sub]
            t = jnp.concatenate([t[:, :sub] + near, t[:, sub : 4 * sub], t[:, 4 * sub :] + far], axis=1)
            top = jnp.max(t, axis=1, keepdims=True)
            p = jnp.exp2((t - top) * LOG2E).astype(BF16)
            groups.append(jnp.concatenate([p, outside] if g % 2 == 0 else [outside, p], axis=1))
        return groups

    steps = [(block, c) for block in blocks for c in range(pairs)]
    later = scores(*steps[0])
    for n, (block, c) in enumerate(steps):
        s = later
        if n + 1 < len(steps):
            later = scores(*steps[n + 1])
        _, _, values, _, store, finish = block
        v = jnp.concatenate([values(c), ones], axis=1)
        w = weights(s)
        heads = [
            jnp.dot(jnp.concatenate(w[2 * h : 2 * h + 2], axis=0), v, preferred_element_type=F32) for h in range(2)
        ]
        o = jnp.concatenate(heads, axis=0)
        o = o[:, :LANES] / o[:, LANES:]
        store(c, jnp.where(first, o[:half], o[half:]).astype(BF16))
        if c == pairs - 1:
            finish()


def decode(x, attended, w_proj, w_fields):
    updated = (x.astype(F32) + jnp.dot(attended, w_proj, preferred_element_type=F32)).astype(BF16)
    return lax.dot_general(w_fields, updated, (((1,), (1,)), ((), ())), preferred_element_type=F32)


def cols(c):
    return slice(c * LANES, (c + 1) * LANES)


def block_of(q, kv, flags, att, q_at, k_at, width, finish):
    def store(c, value):
        att[:, cols(c)] = value

    return (
        lambda c: q[q_at, cols(c)],
        lambda c: kv[k_at, cols(c)],
        lambda c: kv[k_at, slice(width + c * LANES, width + (c + 1) * LANES)],
        flags,
        store,
        finish,
    )


def facing_kernel(x, first, second, sem):
    rows = x.shape[0]
    half = first.shape[0]
    odd = lax.rem(lax.axis_index("node"), 2)
    at = [pl.multiple_of(o * (rows - half), half) for o in (1 - odd, odd)]
    moves = [
        pltpu.make_async_copy(x.at[pl.ds(a, half), :], out, sem.at[i])
        for i, (a, out) in enumerate(zip(at, (first, second)))
    ]
    for c in moves:
        c.start()
    for c in moves:
        c.wait()


def inner_kernel(
    counts, x, pert, gain, w_fields, w_qkv, w_proj, out, q_edge, kv, flags, alive, normed, q_in, att,
):
    rows, width = x.shape
    half = HALF_WINDOW
    blocks = rows // half
    place = lax.axis_index("node")
    shard = iota(counts.shape, 1)

    def count(at):
        return jnp.sum(jnp.where(shard == at, counts[...], 0), axis=1, keepdims=True)

    own, low_live, high_live = count(place), count(place - 1), count(place + 1)
    flags[:half, :] = dead_flags(half, low_live - (rows - half))
    flags[half : half + rows, :] = dead_flags(rows, own)
    flags[half + rows :, :] = dead_flags(half, high_live)
    alive[...] = jnp.where(iota(alive.shape, 1) < own, 1.0, 0.0)
    head_scale = jnp.asarray((width // HEADS) ** -0.5, BF16)

    def part(b):
        return slice(b * half, (b + 1) * half)

    scale = channel_scale(gain, pert)
    normed[part(0), :] = normalize(x[part(0), :], scale)
    for b in range(blocks):
        here = normed[part(b), :]
        for n in range(3):
            res = jnp.dot(here, w_qkv[:, n * width : (n + 1) * width], preferred_element_type=F32).astype(BF16)
            if n > 0:
                kv[part(b), (n - 1) * width : n * width] = res
            elif b == 0:
                q_edge[:half, :] = res * head_scale
            elif b == blocks - 1:
                q_edge[half:, :] = res * head_scale
            else:
                q_in[part(b - 1), :] = res * head_scale
            if n == 0 and b + 1 < blocks:
                normed[part(b + 1), :] = normalize(x[part(b + 1), :], scale)

    def block(b):
        start = b * half

        def finish():
            fields = decode(x[part(b + 1), :], att[b % 2], w_proj[...], w_fields[...])
            live = iota(fields.shape, 1) + start + half < own
            out[:, part(b)] = jnp.where(live, fields, 0.0).astype(BF16)

        window = slice(start, start + 3 * half)
        return block_of(q_in, kv, dead_flags(3 * half, own - start), att.at[b % 2], part(b), window, width, finish)

    attend_blocks([block(b) for b in range(blocks - 2)], width // LANES)


def edge_kernel(
    side, alive, flags, w_fields, x, w_proj, q_edge, kv, *refs,
):
    rows, width = x.shape
    half = HALF_WINDOW
    if side == 0:
        pert, gain, first, second, w_qkv, done, out, halo_high, normed, halo, att = refs
        odd = lax.rem(lax.axis_index("node"), 2)
        scale = channel_scale(gain, pert)
        low = jnp.where(odd == 1, first[...].astype(F32), second[...].astype(F32))
        normed[:half, :] = normalize(low, scale)
        for h, target in enumerate((halo, halo_high)):
            for n in range(2):
                at = slice(n * width, (n + 1) * width)
                w = w_qkv[:, (n + 1) * width : (n + 2) * width]
                rows_in = normed[h * half : (h + 1) * half, :]
                target[:, at] = jnp.dot(rows_in, w, preferred_element_type=F32).astype(BF16)
                if h == 0 and n == 0:
                    high = jnp.where(odd == 1, second[...].astype(F32), first[...].astype(F32))
                    normed[half:, :] = normalize(high, scale)
        near = slice(0, 2 * half)
        out[:, half:] = done[...]
    else:
        halo, out, att = refs
        near = slice(rows - 2 * half, rows)
    start = side * (rows - half)
    here = slice(side * half, (side + 1) * half)

    def window(c):
        parts = [halo[:, cols(c)], kv[near, cols(c)]]
        return jnp.concatenate(parts if side == 0 else parts[::-1], axis=0)

    def store(c, value):
        att[:, cols(c)] = value

    def finish():
        fields = decode(x[start : start + half, :], att[...], w_proj[...], w_fields[...])
        out[:, :half] = jnp.where(alive[:, start : start + half] > 0.0, fields, 0.0).astype(BF16)

    attend_blocks(
        [
            (
                lambda c: q_edge[here, cols(c)],
                window,
                lambda c: window(c + width // LANES),
                flags[start : start + 3 * half, :],
                store,
                finish,
            )
        ],
        width // LANES,
    )


def score_values(mine, others, truth, live):
    total = 1 + len(others)
    eps = (1.0 - alpha_fair) / total
    mine = mine.astype(F32)
    others = [o.astype(F32) for o in others]

    def smooth(d):
        return jnp.sqrt(d * d + smooth_sq)

    d = mine - truth
    a = smooth(d)
    grad = d / a
    truth_sum = a
    for o in others:
        truth_sum = truth_sum + smooth(o - truth)
    pair_sum = jnp.zeros_like(a)
    pair_grad = jnp.zeros_like(a)
    for o in others:
        d = mine - o
        a = smooth(d)
        pair_sum = pair_sum + 2.0 * a
        pair_grad = pair_grad + d / a
    for i in range(len(others)):
        for j in range(i + 1, len(others)):
            pair_sum = pair_sum + 2.0 * smooth(others[i] - others[j])
    score = truth_sum * (1.0 / total) - (1.0 - eps) / (2.0 * total * (total - 1)) * pair_sum
    deriv = grad - (1.0 - eps) / (total - 1) * pair_grad
    return jnp.where(live, score, 0.0), jnp.where(live, deriv, 0.0)


def score_kernel(others, carried, places, alive, *refs):
    mine, rest, truth = refs[0], refs[1 : 1 + others], refs[1 + others]
    pred, score, deriv = refs[2 + others + carried : 5 + others + carried]
    score_buf, deriv_buf, sem = refs[5 + others + carried :]
    half = HALF_WINDOW
    moves = []
    for i, place in enumerate(places):
        here, there = slice(i * half, (i + 1) * half), slice(place * half, (place + 1) * half)
        moves.append(pltpu.make_async_copy(mine.at[:, here], pred.at[:, there], sem.at[0, i]))
        moves[-1].start()
    for i, place in enumerate(places):
        here, there = slice(i * half, (i + 1) * half), slice(place * half, (place + 1) * half)
        f = mine[:, here]
        live = alive[:, there] > 0.0
        score_buf[i], d = score_values(f, [r[:, here] for r in rest], truth[:, there], live)
        moves.append(pltpu.make_async_copy(score_buf.at[i], score.at[:, there], sem.at[1, i]))
        moves[-1].start()
        deriv_buf[i] = d[:, None, :]
        moves.append(pltpu.make_async_copy(deriv_buf.at[i], deriv.at[:, :, there], sem.at[2, i]))
        moves[-1].start()
    for c in moves:
        c.wait()


def score_call(alive, mine, others, truth, carried, places):
    half = HALF_WINDOW
    fields, nodes = truth.shape
    shapes = [
        jax.ShapeDtypeStruct((fields, nodes), BF16),
        jax.ShapeDtypeStruct((fields, nodes), F32),
        jax.ShapeDtypeStruct((fields, 1, nodes), F32),
    ]
    count = len(others)
    parts = len(places)
    return pl.pallas_call(
        functools.partial(score_kernel, count, len(carried), places),
        in_specs=[VMEM] * (3 + count) + [ANY] * len(carried),
        out_specs=[ANY] * 3,
        out_shape=shapes,
        scratch_shapes=[
            pltpu.VMEM((parts, fields, half), F32),
            pltpu.VMEM((parts, fields, 1, half), F32),
            pltpu.SemaphoreType.DMA((3, parts)),
        ],
        compiler_params=pltpu.CompilerParams(vmem_limit_bytes=8 << 20),
        input_output_aliases={3 + count + i: i for i in range(len(carried))},
        cost_estimate=pl.CostEstimate(
            flops=40 * fields * half * parts, bytes_accessed=20 * fields * half * parts, transcendentals=0
        ),
        name="score",
    )(alive, mine, *others, truth, *carried)


def neighbours(count, start):
    pairs = [(i, i + 1) for i in range(start, count - 1, 2)]
    return pairs + [(t, s) for s, t in pairs]


def on_device(hidden, pert, gain, w_qkv, w_proj, w_fields, truth, counts):
    _, rows, width = hidden.shape
    fields = w_fields.shape[1]
    half = HALF_WINDOW
    blocks = rows // half
    x = hidden[0]
    gain = gain.reshape(1, width)
    w_fields = w_fields.T
    shards = lax.axis_size("node")
    members = lax.axis_size("ens")
    halves = pl.pallas_call(
        facing_kernel,
        in_specs=[ANY],
        out_specs=[VMEM] * 2,
        out_shape=[jax.ShapeDtypeStruct((half, width), BF16)] * 2,
        scratch_shapes=[pltpu.SemaphoreType.DMA((2,))],
        compiler_params=pltpu.CompilerParams(vmem_limit_bytes=4 << 20),
        cost_estimate=pl.CostEstimate(flops=FACING_FLOPS, bytes_accessed=4 * half * width, transcendentals=0),
        name="facing",
    )(pltpu.with_memory_space_constraint(x, pltpu.HBM))
    first = lax.ppermute(halves[0], "node", neighbours(shards, 0))
    second = lax.ppermute(halves[1], "node", neighbours(shards, 1))

    inner = rows - 2 * half
    pred_in, q_edge, kv, flags, alive = pl.pallas_call(
        inner_kernel,
        in_specs=[VMEM] * 7,
        out_specs=[VMEM] * 5,
        out_shape=[
            jax.ShapeDtypeStruct((fields, inner), BF16),
            jax.ShapeDtypeStruct((2 * half, width), BF16),
            jax.ShapeDtypeStruct((rows, 2 * width), BF16),
            jax.ShapeDtypeStruct((rows + 2 * half, LANES), BF16),
            jax.ShapeDtypeStruct((1, rows), F32),
        ],
        scratch_shapes=[
            pltpu.VMEM((rows, width), BF16),
            pltpu.VMEM((inner, width), BF16),
            pltpu.VMEM((2, half, width), BF16),
        ],
        compiler_params=pltpu.CompilerParams(vmem_limit_bytes=KERNEL_VMEM),
        cost_estimate=pl.CostEstimate(
            flops=2 * rows * width * 3 * width + 2 * inner * width * width + 12 * inner * width * half,
            bytes_accessed=10 * width * width,
            transcendentals=inner * HEADS * 3 * half,
        ),
        name="inner_blocks",
    )(counts.reshape(1, -1), x, pert, gain, w_fields, w_qkv, w_proj)

    def exchange(part):
        return [
            lax.ppermute(part, "ens", [(i, (i + s) % members) for i in range(members)])
            for s in range(1, members)
        ]

    def edge(side, out_shape, scratch, flops, *extra):
        return pl.pallas_call(
            functools.partial(edge_kernel, side),
            in_specs=[VMEM] * (7 + len(extra)),
            out_specs=[VMEM] * len(out_shape),
            out_shape=[jax.ShapeDtypeStruct(shape, BF16) for shape in out_shape],
            scratch_shapes=[pltpu.VMEM(shape, BF16) for shape in scratch],
            compiler_params=pltpu.CompilerParams(vmem_limit_bytes=KERNEL_VMEM),
            cost_estimate=pl.CostEstimate(
                flops=flops + 12 * half * width * half,
                bytes_accessed=10 * width * width,
                transcendentals=half * HEADS * 3 * half,
            ),
            name="edge_block",
        )(alive, flags, w_fields, x, w_proj, q_edge, kv, *extra)

    pred_most, halo_high = edge(
        0,
        [(fields, rows - half), (half, 2 * width)],
        [(2 * half, width), (half, 2 * width), (half, width)],
        10 * half * width * width,
        pert, gain, first, second, w_qkv, pred_in,
    )
    others_most = exchange(pred_most)
    (pred_last,) = edge(1, [(fields, half)], [(half, width)], 2 * half * width * width, halo_high)
    others_last = exchange(pred_last)
    partial = score_call(alive, pred_most, others_most, truth, [], list(range(blocks - 1)))
    pred, score, deriv = score_call(alive, pred_last, others_last, truth, partial, [blocks - 1])
    return pred[None], score, deriv.transpose(1, 0, 2)


def solution(mesh):
    return jax.shard_map(
        on_device,
        mesh=mesh,
        in_specs=(P("ens", "node", None), P("ens", None), P(), P(), P(), P(), P(None, "node"), P()),
        out_specs=(P("ens", None, "node"), P(None, "node"), P("ens", None, "node")),
        check_vma=False,
    )
```

```python
import functools

import jax
import jax.numpy as jnp
from jax import lax
from jax.experimental import pallas as pl
from jax.experimental.pallas import tpu as pltpu
from jax.sharding import PartitionSpec as P

HEADS = 16
HALF_WINDOW = 256
LANES = 128

smooth_sq = 0.01
alpha_fair = 0.95
NEG = -1e30
LOG2E = 1.4426950408889634
KERNEL_VMEM = 32 << 20
FACING_FLOPS = 8_000_000_000

F32 = jnp.float32
BF16 = jnp.bfloat16
VMEM = pl.BlockSpec(memory_space=pltpu.VMEM)
ANY = pl.BlockSpec(memory_space=pl.ANY)


def iota(shape, dim):
    return lax.broadcasted_iota(jnp.int32, shape, dim)


def normalize(x, scale):
    x32 = x.astype(F32)
    mean = jnp.mean(x32, axis=-1, keepdims=True)
    centred = x32 - mean
    var = jnp.mean(centred * centred, axis=-1, keepdims=True)
    return (centred * lax.rsqrt(var + 1e-05) * scale).astype(BF16)


def channel_scale(gain_ref, pert_ref):
    return gain_ref[...] * (1.0 + pert_ref[...].astype(F32))


def dead_flags(rows, live):
    return jnp.where((iota((rows, LANES), 0) >= live) & (iota((rows, LANES), 1) == 0), 1.0, 0.0).astype(BF16)


def attend_blocks(blocks, pairs):
    half = HALF_WINDOW
    sub = half // 2
    row = iota((sub, sub), 0)
    col = iota((sub, sub), 1)
    near = jnp.where(col >= row, 0.0, NEG)
    far = jnp.where(col < row, 0.0, NEG)
    bias = jnp.where(iota((2 * half, LANES), 1) == 0, NEG, 0.0).astype(BF16)
    ones = jnp.ones((3 * half, LANES), BF16)
    outside = jnp.zeros((sub, sub), BF16)
    lane = iota((half, LANES), 1)
    first = lane < LANES // 2

    def scores(block, c):
        query, keys, _, flags, _, _ = block
        q = query(c)
        zero = jnp.zeros_like(q)
        both = jnp.concatenate([jnp.where(first, q, zero), jnp.where(first, zero, q)], axis=0)
        both = jnp.concatenate([both, bias], axis=1)
        k = jnp.concatenate([keys(c), flags], axis=1)
        return lax.dot_general(both, k, (((1,), (1,)), ((), ())), preferred_element_type=F32)

    def weights(s):
        groups = []
        for g in range(4):
            t = s[g * sub : (g + 1) * sub, (g % 2) * sub : (g % 2) * sub + 5 * sub]
            t = jnp.concatenate([t[:, :sub] + near, t[:, sub : 4 * sub], t[:, 4 * sub :] + far], axis=1)
            top = jnp.max(t, axis=1, keepdims=True)
            p = jnp.exp2((t - top) * LOG2E).astype(BF16)
            groups.append(jnp.concatenate([p, outside] if g % 2 == 0 else [outside, p], axis=1))
        return groups

    steps = [(block, c) for block in blocks for c in range(pairs)]
    later = scores(*steps[0])
    for n, (block, c) in enumerate(steps):
        s = later
        if n + 1 < len(steps):
            later = scores(*steps[n + 1])
        _, _, values, _, store, finish = block
        v = jnp.concatenate([values(c), ones], axis=1)
        w = weights(s)
        heads = [
            jnp.dot(jnp.concatenate(w[2 * h : 2 * h + 2], axis=0), v, preferred_element_type=F32) for h in range(2)
        ]
        o = jnp.concatenate(heads, axis=0)
        o = o[:, :LANES] / o[:, LANES:]
        store(c, jnp.where(first, o[:half], o[half:]).astype(BF16))
        if c == pairs - 1:
            finish()


def decode(x, attended, w_proj, w_fields):
    updated = (x.astype(F32) + jnp.dot(attended, w_proj, preferred_element_type=F32)).astype(BF16)
    return lax.dot_general(w_fields, updated, (((1,), (1,)), ((), ())), preferred_element_type=F32)


def cols(c):
    return slice(c * LANES, (c + 1) * LANES)


def block_of(q, kv, flags, att, q_at, k_at, width, finish):
    def store(c, value):
        att[:, cols(c)] = value

    return (
        lambda c: q[q_at, cols(c)],
        lambda c: kv[k_at, cols(c)],
        lambda c: kv[k_at, slice(width + c * LANES, width + (c + 1) * LANES)],
        flags,
        store,
        finish,
    )


def facing_kernel(x, first, second, sem):
    rows = x.shape[0]
    half = first.shape[0]
    odd = lax.rem(lax.axis_index("node"), 2)
    at = [pl.multiple_of(o * (rows - half), half) for o in (1 - odd, odd)]
    moves = [
        pltpu.make_async_copy(x.at[pl.ds(a, half), :], out, sem.at[i])
        for i, (a, out) in enumerate(zip(at, (first, second)))
    ]
    for c in moves:
        c.start()
    for c in moves:
        c.wait()


def inner_kernel(
    counts, x, pert, gain, w_fields, w_qkv, w_proj, out, q_edge, kv, flags, alive, normed, q_in, att,
):
    rows, width = x.shape
    half = HALF_WINDOW
    blocks = rows // half
    place = lax.axis_index("node")
    shard = iota(counts.shape, 1)

    def count(at):
        return jnp.sum(jnp.where(shard == at, counts[...], 0), axis=1, keepdims=True)

    own, low_live, high_live = count(place), count(place - 1), count(place + 1)
    flags[:half, :] = dead_flags(half, low_live - (rows - half))
    flags[half : half + rows, :] = dead_flags(rows, own)
    flags[half + rows :, :] = dead_flags(half, high_live)
    alive[...] = jnp.where(iota(alive.shape, 1) < own, 1.0, 0.0)
    head_scale = jnp.asarray((width // HEADS) ** -0.5, BF16)

    def part(b):
        return slice(b * half, (b + 1) * half)

    scale = channel_scale(gain, pert)
    normed[part(0), :] = normalize(x[part(0), :], scale)
    for b in range(blocks):
        here = normed[part(b), :]
        for n in range(3):
            res = jnp.dot(here, w_qkv[:, n * width : (n + 1) * width], preferred_element_type=F32).astype(BF16)
            if n > 0:
                kv[part(b), (n - 1) * width : n * width] = res
            elif b == 0:
                q_edge[:half, :] = res * head_scale
            elif b == blocks - 1:
                q_edge[half:, :] = res * head_scale
            else:
                q_in[part(b - 1), :] = res * head_scale
            if n == 0 and b + 1 < blocks:
                normed[part(b + 1), :] = normalize(x[part(b + 1), :], scale)

    def block(b):
        start = b * half

        def finish():
            fields = decode(x[part(b + 1), :], att[b % 2], w_proj[...], w_fields[...])
            live = iota(fields.shape, 1) + start + half < own
            out[:, part(b)] = jnp.where(live, fields, 0.0).astype(BF16)

        window = slice(start, start + 3 * half)
        return block_of(q_in, kv, dead_flags(3 * half, own - start), att.at[b % 2], part(b), window, width, finish)

    attend_blocks([block(b) for b in range(blocks - 2)], width // LANES)


def edge_kernel(
    side, alive, flags, w_fields, x, w_proj, q_edge, kv, *refs,
):
    rows, width = x.shape
    half = HALF_WINDOW
    if side == 0:
        pert, gain, first, second, w_qkv, done, out, halo_high, normed, halo, att = refs
        odd = lax.rem(lax.axis_index("node"), 2)
        scale = channel_scale(gain, pert)
        low = jnp.where(odd == 1, first[...].astype(F32), second[...].astype(F32))
        normed[:half, :] = normalize(low, scale)
        for h, target in enumerate((halo, halo_high)):
            for n in range(2):
                at = slice(n * width, (n + 1) * width)
                w = w_qkv[:, (n + 1) * width : (n + 2) * width]
                rows_in = normed[h * half : (h + 1) * half, :]
                target[:, at] = jnp.dot(rows_in, w, preferred_element_type=F32).astype(BF16)
                if h == 0 and n == 0:
                    high = jnp.where(odd == 1, second[...].astype(F32), first[...].astype(F32))
                    normed[half:, :] = normalize(high, scale)
        near = slice(0, 2 * half)
        out[:, half:] = done[...]
    else:
        halo, out, att = refs
        near = slice(rows - 2 * half, rows)
    start = side * (rows - half)
    here = slice(side * half, (side + 1) * half)

    def window(c):
        parts = [halo[:, cols(c)], kv[near, cols(c)]]
        return jnp.concatenate(parts if side == 0 else parts[::-1], axis=0)

    def store(c, value):
        att[:, cols(c)] = value

    def finish():
        fields = decode(x[start : start + half, :], att[...], w_proj[...], w_fields[...])
        out[:, :half] = jnp.where(alive[:, start : start + half] > 0.0, fields, 0.0).astype(BF16)

    attend_blocks(
        [
            (
                lambda c: q_edge[here, cols(c)],
                window,
                lambda c: window(c + width // LANES),
                flags[start : start + 3 * half, :],
                store,
                finish,
            )
        ],
        width // LANES,
    )


def score_values(mine, others, truth, live):
    total = 1 + len(others)
    eps = (1.0 - alpha_fair) / total
    mine = mine.astype(F32)
    others = [o.astype(F32) for o in others]

    def smooth(d):
        return jnp.sqrt(d * d + smooth_sq)

    d = mine - truth
    a = smooth(d)
    grad = d / a
    truth_sum = a
    for o in others:
        truth_sum = truth_sum + smooth(o - truth)
    pair_sum = jnp.zeros_like(a)
    pair_grad = jnp.zeros_like(a)
    for o in others:
        d = mine - o
        a = smooth(d)
        pair_sum = pair_sum + 2.0 * a
        pair_grad = pair_grad + d / a
    for i in range(len(others)):
        for j in range(i + 1, len(others)):
            pair_sum = pair_sum + 2.0 * smooth(others[i] - others[j])
    score = truth_sum * (1.0 / total) - (1.0 - eps) / (2.0 * total * (total - 1)) * pair_sum
    deriv = grad - (1.0 - eps) / (total - 1) * pair_grad
    return jnp.where(live, score, 0.0), jnp.where(live, deriv, 0.0)


def score_kernel(others, carried, places, alive, *refs):
    mine, rest, truth = refs[0], refs[1 : 1 + others], refs[1 + others]
    refs = refs[2 + others :]
    half = HALF_WINDOW
    moves = []
    if carried:
        score, deriv, score_buf, deriv_buf, sem = refs[carried:]
    else:
        last, pred, score, deriv, score_buf, deriv_buf, sem = refs
        split = mine.shape[1]
        moves.append(pltpu.make_async_copy(mine, pred.at[:, :split], sem.at[2, 0]))
        moves.append(pltpu.make_async_copy(last, pred.at[:, split:], sem.at[2, 1]))
        for c in moves:
            c.start()
    for i, place in enumerate(places):
        here, there = slice(i * half, (i + 1) * half), slice(place * half, (place + 1) * half)
        live = alive[:, there] > 0.0
        score_buf[i], d = score_values(mine[:, here], [r[:, here] for r in rest], truth[:, there], live)
        moves.append(pltpu.make_async_copy(score_buf.at[i], score.at[:, there], sem.at[0, i]))
        moves[-1].start()
        deriv_buf[i] = d[:, None, :]
        moves.append(pltpu.make_async_copy(deriv_buf.at[i], deriv.at[:, :, there], sem.at[1, i]))
        moves[-1].start()
    for c in moves:
        c.wait()


def score_call(alive, mine, others, truth, carried, places, *last):
    half = HALF_WINDOW
    fields, nodes = truth.shape
    shapes = [jax.ShapeDtypeStruct((fields, nodes), BF16)] * len(last) + [
        jax.ShapeDtypeStruct((fields, nodes), F32),
        jax.ShapeDtypeStruct((fields, 1, nodes), F32),
    ]
    count = len(others)
    parts = len(places)
    return pl.pallas_call(
        functools.partial(score_kernel, count, len(carried), places),
        in_specs=[VMEM] * (3 + count + len(last)) + [ANY] * len(carried),
        out_specs=[ANY] * len(shapes),
        out_shape=shapes,
        scratch_shapes=[
            pltpu.VMEM((parts, fields, half), F32),
            pltpu.VMEM((parts, fields, 1, half), F32),
            pltpu.SemaphoreType.DMA((3, max(parts, 2))),
        ],
        compiler_params=pltpu.CompilerParams(vmem_limit_bytes=8 << 20),
        input_output_aliases={3 + count + i: i for i in range(len(carried))},
        cost_estimate=pl.CostEstimate(
            flops=40 * fields * half * parts, bytes_accessed=20 * fields * half * parts, transcendentals=0
        ),
        name="score",
    )(alive, mine, *others, truth, *last, *carried)


def neighbours(count, start):
    pairs = [(i, i + 1) for i in range(start, count - 1, 2)]
    return pairs + [(t, s) for s, t in pairs]


def on_device(hidden, pert, gain, w_qkv, w_proj, w_fields, truth, counts):
    _, rows, width = hidden.shape
    fields = w_fields.shape[1]
    half = HALF_WINDOW
    blocks = rows // half
    x = hidden[0]
    gain = gain.reshape(1, width)
    w_fields = w_fields.T
    shards = lax.axis_size("node")
    members = lax.axis_size("ens")
    halves = pl.pallas_call(
        facing_kernel,
        in_specs=[ANY],
        out_specs=[VMEM] * 2,
        out_shape=[jax.ShapeDtypeStruct((half, width), BF16)] * 2,
        scratch_shapes=[pltpu.SemaphoreType.DMA((2,))],
        compiler_params=pltpu.CompilerParams(vmem_limit_bytes=4 << 20),
        cost_estimate=pl.CostEstimate(flops=FACING_FLOPS, bytes_accessed=4 * half * width, transcendentals=0),
        name="facing",
    )(pltpu.with_memory_space_constraint(x, pltpu.HBM))
    first = lax.ppermute(halves[0], "node", neighbours(shards, 0))
    second = lax.ppermute(halves[1], "node", neighbours(shards, 1))

    inner = rows - 2 * half
    pred_in, q_edge, kv, flags, alive = pl.pallas_call(
        inner_kernel,
        in_specs=[VMEM] * 7,
        out_specs=[VMEM] * 5,
        out_shape=[
            jax.ShapeDtypeStruct((fields, inner), BF16),
            jax.ShapeDtypeStruct((2 * half, width), BF16),
            jax.ShapeDtypeStruct((rows, 2 * width), BF16),
            jax.ShapeDtypeStruct((rows + 2 * half, LANES), BF16),
            jax.ShapeDtypeStruct((1, rows), F32),
        ],
        scratch_shapes=[
            pltpu.VMEM((rows, width), BF16),
            pltpu.VMEM((inner, width), BF16),
            pltpu.VMEM((2, half, width), BF16),
        ],
        compiler_params=pltpu.CompilerParams(vmem_limit_bytes=KERNEL_VMEM),
        cost_estimate=pl.CostEstimate(
            flops=2 * rows * width * 3 * width + 2 * inner * width * width + 12 * inner * width * half,
            bytes_accessed=10 * width * width,
            transcendentals=inner * HEADS * 3 * half,
        ),
        name="inner_blocks",
    )(counts.reshape(1, -1), x, pert, gain, w_fields, w_qkv, w_proj)

    def exchange(part):
        return [
            lax.ppermute(part, "ens", [(i, (i + s) % members) for i in range(members)])
            for s in range(1, members)
        ]

    def edge(side, out_shape, scratch, flops, *extra):
        return pl.pallas_call(
            functools.partial(edge_kernel, side),
            in_specs=[VMEM] * (7 + len(extra)),
            out_specs=[VMEM] * len(out_shape),
            out_shape=[jax.ShapeDtypeStruct(shape, BF16) for shape in out_shape],
            scratch_shapes=[pltpu.VMEM(shape, BF16) for shape in scratch],
            compiler_params=pltpu.CompilerParams(vmem_limit_bytes=KERNEL_VMEM),
            cost_estimate=pl.CostEstimate(
                flops=flops + 12 * half * width * half,
                bytes_accessed=10 * width * width,
                transcendentals=half * HEADS * 3 * half,
            ),
            name="edge_block",
        )(alive, flags, w_fields, x, w_proj, q_edge, kv, *extra)

    pred_most, halo_high = edge(
        0,
        [(fields, rows - half), (half, 2 * width)],
        [(2 * half, width), (half, 2 * width), (half, width)],
        10 * half * width * width,
        pert, gain, first, second, w_qkv, pred_in,
    )
    others_most = exchange(pred_most)
    (pred_last,) = edge(1, [(fields, half)], [(half, width)], 2 * half * width * width, halo_high)
    others_last = exchange(pred_last)
    places = list(range(blocks - 1))
    pred, *partial = score_call(alive, pred_most, others_most, truth, [], places, pred_last)
    score, deriv = score_call(alive, pred_last, others_last, truth, partial, [blocks - 1])
    return pred[None], score, deriv.transpose(1, 0, 2)


def solution(mesh):
    return jax.shard_map(
        on_device,
        mesh=mesh,
        in_specs=(P("ens", "node", None), P("ens", None), P(), P(), P(), P(), P(None, "node"), P()),
        out_specs=(P("ens", None, "node"), P(None, "node"), P("ens", None, "node")),
        check_vma=False,
    )
```
